32 devices in a mesh: grp: 2 (over y), gx: 16 (over z, x, core).
Axes of the slice: x: 2, y: 2, z: 4, core: 2. Of those that a mesh axis runs over, the one named last changes fastest.
Arguments:
- activations: bfloat16 [4, 32, 64, 4, 1024], P('grp', None, 'gx'), parts along dimension 0, may hold values from -6 to 6
- cotangent: bfloat16 [4, 32, 64, 4, 1024], P('grp', None, 'gx'), parts along dimension 0, may hold values from -6 to 6
- kernel: bfloat16 [32, 32, 3, 3, 3], replicated, may hold values from -0.21875 to 0.21875
- channel_bias: float32 [32], replicated, may hold values from -3 to 3
Outputs:
- activated: bfloat16 [4, 32, 64, 4, 1024], P('grp', None, 'gx'), parts along dimension 0
- grad_input: bfloat16 [4, 32, 64, 4, 1024], P('grp', None, 'gx'), parts along dimension 0
- grad_kernel: float32 [64, 32, 3, 3, 3], P('grp'), parts along dimension 0
- grad_bias: float32 [64], P('grp'), parts along dimension 0
The draws below stay inside these ranges and needn't reach their ends.
There are 2 independent parts, one for each index of `grp`. The reference program is written for one: setup_inputs(seed, part) draws one part's arguments, and reference() takes and returns one part's arrays. A program takes and returns all parts, laid end to end along the dimension named above; an argument that names none is the same for every part. Nothing has to cross between parts.
All inputs are finite; a program needn't handle non-finite values.
Results may differ from the reference program's by a relative error of at most 0.0055.
Values may be sent and summed in bfloat16 or wider, within the bound.
A program may use at most 256 MiB of HBM per device.

```python
import jax
import jax.numpy as jnp
from jax import lax

C = 32
B = 2
YB = 4
Z = 1024
NX = 64


def block_scale(own_key, extent, pieces, low, top_value):
    def one(axis_at, parts):
        steps = jax.random.uniform(jax.random.fold_in(jax.random.fold_in(own_key, 6), axis_at), (parts,), jnp.float32, low / len(pieces), top_value / len(pieces))
        return jnp.repeat(jnp.exp(steps), extent[axis_at] // parts).reshape((-1,) + (1,) * (len(extent) - axis_at - 1))

    loudness = one(*pieces[0])
    for cut in pieces[1:]:
        loudness = loudness * one(*cut)
    return loudness


def scatter_about(rng, dims, scale, most, split=(), kind=jnp.bfloat16):
    drawn = scale * jax.random.normal(rng, dims, jnp.float32)
    if split:
        drawn = drawn * block_scale(rng, dims, split, -0.22, 0.18)
    return jnp.clip(drawn, -most, most).astype(kind)


def setup_inputs(seed: int = 0, part: int = 0) -> dict:
    splits = jax.random.split(jax.random.key(seed), 5)
    own_keys = jax.random.split(jax.random.fold_in(splits[4], part), 5)
    return {
        "activations": scatter_about(own_keys[0], (B, C, NX, YB, Z), 1.0, 6.0, ((2, 16),)),
        "cotangent": scatter_about(own_keys[1], (B, C, NX, YB, Z), 1.0, 6.0, ((2, 16),)),
        "kernel": scatter_about(splits[2], (C, C, 3, 3, 3), (27 * C) ** -0.5, 0.21875),
        "channel_bias": scatter_about(splits[3], (C,), 0.5, 3.0, (), jnp.float32),
    }


def convolve(source, filters, xpad):
    return lax.conv_general_dilated(source, filters, (1, 1, 1), ((xpad, xpad), (1, 1), (1, 1)), dimension_numbers=("NCDHW", "OIDHW", "NCDHW"), preferred_element_type=jnp.float32)


def gelu_parts(before):
    cumulative = 0.5 * (1.0 + lax.erf(before * 0.7071067811865476))
    density = jnp.exp(-0.5 * before * before) * 0.3989422804014327
    return before * cumulative, cumulative + before * density


def reference(activations, cotangent, kernel, channel_bias):
    before = convolve(activations, kernel, 1) + channel_bias.astype(jnp.float32)[None, :, None, None, None]
    activated_full, derivative = gelu_parts(before)
    activated = activated_full.astype(jnp.bfloat16)
    delta = (cotangent.astype(jnp.float32) * derivative).astype(jnp.bfloat16)
    flipped = jnp.transpose(kernel[:, :, ::-1, ::-1, ::-1], (1, 0, 2, 3, 4))
    grad_input = convolve(delta, flipped, 1).astype(jnp.bfloat16)
    normalizer = float(B * NX * YB * Z) ** -0.5
    padded = jnp.pad(activations, ((0, 0), (0, 0), (1, 1), (1, 1), (1, 1))).astype(jnp.float32)
    delta_wide = delta.astype(jnp.float32)
    nx_cells = delta.shape[2]
    rows = []
    for offset_i in range(3):
        for offset_j in range(3):
            for offset_k in range(3):
                window = padded[:, :, offset_i:offset_i + nx_cells, offset_j:offset_j + YB, offset_k:offset_k + Z]
                rows.append(jnp.einsum("bcxyz,boxyz->oc", window, delta_wide))
    stacked = jnp.stack(rows, axis=-1).reshape(C, C, 3, 3, 3)
    grad_kernel = stacked * normalizer
    grad_bias = jnp.sum(delta_wide, axis=(0, 2, 3, 4)) * normalizer
    return activated, grad_input, grad_kernel, grad_bias
```

```python
import functools

import jax
import jax.numpy as jnp
from jax import lax
from jax.experimental import pallas as pl
from jax.experimental.pallas import tpu as pltpu
from jax.sharding import PartitionSpec as P

F32 = jnp.float32
BF16 = jnp.bfloat16
MESH = pl.DeviceIdType.MESH
NT = (((1,), (1,)), ((), ()))
ZC = 256


def one_hot_rows(rows, group, dtype):
    r = lax.broadcasted_iota(jnp.int32, (rows, rows // group), 0)
    c = lax.broadcasted_iota(jnp.int32, (rows, rows // group), 1)
    return jnp.where(r // group == c, 1.0, 0.0).astype(dtype)


def one_hot_cols(rows, group, dtype):
    r = lax.broadcasted_iota(jnp.int32, (rows // group, rows), 0)
    c = lax.broadcasted_iota(jnp.int32, (rows // group, rows), 1)
    return jnp.where(c // group == r, 1.0, 0.0).astype(dtype)


def shifted(v):
    zero = jnp.zeros((v.shape[0], 1), v.dtype)
    return (
        jnp.concatenate([zero, v[:, :-1]], axis=1),
        jnp.concatenate([v[:, 1:], zero], axis=1),
    )


def build_weights(taps_ref, w_ref, w_back_ref, rows, yb):
    c = rows // yb
    spread_rows = one_hot_rows(rows, yb, BF16)
    spread_cols = one_hot_cols(rows, yb, BF16)
    r = lax.broadcasted_iota(jnp.int32, (rows, rows), 0)
    s = lax.broadcasted_iota(jnp.int32, (rows, rows), 1)
    offset = s % yb - r % yb
    wide = jnp.dot(taps_ref[...].reshape(27 * c, c), spread_cols, preferred_element_type=F32).astype(BF16)
    w_ref[...] = jnp.zeros_like(w_ref)
    w_back_ref[...] = jnp.zeros_like(w_back_ref)
    for i in range(3):
        for k in range(3):
            block = jnp.zeros((rows, rows), F32)
            for j in range(3):
                tap = (i * 3 + j) * 3 + k
                full = jnp.dot(spread_rows, wide[tap * c:(tap + 1) * c], preferred_element_type=F32)
                block = jnp.where(offset == j - 1, full, block)
            back = block.T.astype(BF16)
            block = block.astype(BF16)
            for xo in range(2):
                at = slice(xo * rows, (xo + 1) * rows)
                ahead = ((xo + i) * 3 + k) * rows
                behind = ((xo + 2 - i) * 3 + k) * rows
                w_ref[at, ahead:ahead + rows] = block
                w_back_ref[at, behind:behind + rows] = back


def main_kernel(act_ref, cot_ref, taps_ref, bias_ref, activated_ref, grad_ref, sums_ref,
                act_v, cot_v, halo, s_ref, d_ref, activated_v, grad_v, w_ref, w_back_ref,
                acc_ref, fold_ref, parts, received, mine, gathered,
                load_sem, face_send, face_recv, delta_send, delta_recv, out_sem,
                send1, recv1, send2, recv2, *, n, scale):
    nb, c, nx, yb, z = act_v.shape
    rows = c * yb
    me = lax.axis_index("gx")
    up, down = lax.rem(me + 1, n), lax.rem(me + n - 1, n)
    has_down, has_up = me > 0, me < n - 1

    def load(b):
        return (pltpu.make_async_copy(act_ref.at[b], act_v.at[b], load_sem.at[0, b]),
                pltpu.make_async_copy(cot_ref.at[b], cot_v.at[b], load_sem.at[1, b]))

    def face(side, b):
        return pltpu.make_async_remote_copy(
            src_ref=act_ref.at[b, :, nx - 1 if side == 0 else 0], dst_ref=halo.at[side, b],
            send_sem=face_send.at[side, b], recv_sem=face_recv.at[side, b],
            device_id={"gx": up if side == 0 else down}, device_id_type=MESH)

    def centre(slot):
        return pl.ds((slot * 3 + 1) * rows, rows)

    def delta(side, b):
        return pltpu.make_async_remote_copy(
            src_ref=d_ref.at[b, centre(nx if side == 0 else 1)],
            dst_ref=d_ref.at[b, centre(0 if side == 0 else nx + 1)],
            send_sem=delta_send.at[side, b], recv_sem=delta_recv.at[side, b],
            device_id={"gx": up if side == 0 else down}, device_id_type=MESH)

    def start_both(copy, b):
        @pl.when(has_up)
        def _():
            copy(0, b).start()

        @pl.when(has_down)
        def _():
            copy(1, b).start()

    def received_both(copy, b):
        @pl.when(has_down)
        def _():
            copy(0, b).wait_recv()

        @pl.when(has_up)
        def _():
            copy(1, b).wait_recv()

    def sent_both(copy, b):
        @pl.when(has_up)
        def _():
            copy(0, b).wait_send()

        @pl.when(has_down)
        def _():
            copy(1, b).wait_send()

    def result(which, b):
        src, dst = ((activated_v, activated_ref), (grad_v, grad_ref))[which]
        return pltpu.make_async_copy(src.at[b], dst.at[b], out_sem.at[which, b])

    def each(f):
        def step(d, carry):
            f(d, lax.rem(me + d, n), lax.rem(me + n - d, n))
            return carry
        lax.fori_loop(1, n, step, 0)

    def scatter(d, owner):
        return pltpu.make_async_remote_copy(
            src_ref=parts.at[owner], dst_ref=received.at[d - 1], send_sem=send1.at[d - 1], recv_sem=recv1.at[d - 1],
            device_id={"gx": owner}, device_id_type=MESH)

    def spread(d, slot, peer):
        return pltpu.make_async_remote_copy(
            src_ref=mine, dst_ref=gathered.at[slot], send_sem=send2.at[d - 1], recv_sem=recv2.at[d - 1],
            device_id={"gx": peer}, device_id_type=MESH)

    def over_samples(f):
        def step(b, carry):
            f(b)
            return carry
        lax.fori_loop(0, nb, step, 0)

    for b in range(nb):
        for copy in load(b):
            copy.start()
    barrier = pltpu.get_barrier_semaphore()
    each(lambda d, to, source: pl.semaphore_signal(barrier, inc=1, device_id={"gx": to}, device_id_type=MESH))
    pl.semaphore_wait(barrier, n - 1)
    for b in range(nb):
        start_both(face, b)

    @pl.when(me == 0)
    def _():
        for b in range(nb):
            halo[0, b] = jnp.zeros((c, yb, z), BF16)
            d_ref[b, centre(0)] = jnp.zeros((rows, z), BF16)

    @pl.when(me == n - 1)
    def _():
        for b in range(nb):
            halo[1, b] = jnp.zeros((c, yb, z), BF16)
            d_ref[b, centre(nx + 1)] = jnp.zeros((rows, z), BF16)

    build_weights(taps_ref, w_ref, w_back_ref, rows, yb)
    column = jnp.sum(one_hot_rows(rows, yb, F32) * bias_ref[...], axis=1, keepdims=True)

    def fill(b, slot, v):
        before, after = shifted(v)
        for k, part in enumerate((before, v, after)):
            s_ref[b, pl.ds((slot * 3 + k) * rows, rows)] = part

    def shift_delta(b, slot):
        before, after = shifted(d_ref[b, centre(slot)])
        d_ref[b, pl.ds(slot * 3 * rows, rows)] = after
        d_ref[b, pl.ds((slot * 3 + 2) * rows, rows)] = before

    def forward(b, x, width):
        depth = (width + 2) * 3 * rows
        for m in range(z // ZC):
            zs = slice(m * ZC, (m + 1) * ZC)
            pre = jnp.dot(w_ref[0:width * rows, 0:depth], s_ref[b, pl.ds(x * 3 * rows, depth), zs],
                          preferred_element_type=F32)
            for xo in range(width):
                t = pre[xo * rows:(xo + 1) * rows] + column
                cumulative = 0.5 * (1.0 + lax.erf(t * 0.7071067811865476))
                density = jnp.exp(-0.5 * t * t) * 0.3989422804014327
                activated_v[b, :, x + xo, :, zs] = (t * cumulative).astype(BF16).reshape(c, yb, ZC)
                g = cot_v[b, :, x + xo, :, zs].reshape(rows, ZC).astype(F32)
                d_ref[b, centre(x + xo + 1), zs] = (g * (cumulative + t * density)).astype(BF16)

    def backward(b, x, width):
        depth = (width + 2) * 3 * rows
        for m in range(z // ZC):
            zs = slice(m * ZC, (m + 1) * ZC)
            g = jnp.dot(w_back_ref[0:width * rows, 0:depth], d_ref[b, pl.ds(x * 3 * rows, depth), zs],
                        preferred_element_type=F32)
            for xo in range(width):
                part = g[xo * rows:(xo + 1) * rows].astype(BF16)
                grad_v[b, :, x + xo, :, zs] = part.reshape(c, yb, ZC)

    def inner(b):
        for copy in load(b):
            copy.wait()
        for x in range(nx):
            fill(b, x + 1, act_v[b, :, x].reshape(rows, z))
        for x in range(1, nx - 1, 2):
            forward(b, x, 2)
        for x in range(1, nx - 1):
            shift_delta(b, x + 1)

    over_samples(inner)
    acc_ref[...] = jnp.zeros_like(acc_ref)

    def outer(b):
        received_both(face, b)
        fill(b, 0, halo[0, b].reshape(rows, z))
        fill(b, nx + 1, halo[1, b].reshape(rows, z))
        forward(b, 0, 1)
        forward(b, nx - 1, 1)
        start_both(delta, b)
        result(0, b).start()
        shift_delta(b, 1)
        shift_delta(b, nx)
        for x in range(nx):
            planes = [s_ref[b, centre(x + i)] for i in range(3)]
            right = jnp.concatenate(planes + [jnp.ones((rows, z), BF16)], axis=0)
            product = lax.dot_general(d_ref[b, pl.ds((x + 1) * 3 * rows, 3 * rows)], right, NT,
                                      preferred_element_type=F32)
            for i in range(4):
                acc_ref[i] += product[:, i * rows:(i + 1) * rows]

    over_samples(outer)

    lane = lax.broadcasted_iota(jnp.int32, (c, rows), 1)
    row = lax.broadcasted_iota(jnp.int32, (c, rows), 0)

    def place(tap, value):
        at, col = tap // 4 * c, tap % 4 * rows
        fold_ref[at:at + c, col:col + rows] = value

    for i in range(3):
        for k in range(3):
            lines = [acc_ref[i, pl.ds(k * rows + y, c, stride=yb), :] for y in range(yb)]
            for j in range(3):
                value = jnp.zeros((c, rows), F32)
                for y in range(yb):
                    if 0 <= y + j - 1 < yb:
                        value = jnp.where(lane % yb == y + j - 1, lines[y], value)
                place((i * 3 + j) * 3 + k, value)
    total = jnp.zeros((c, rows), F32)
    for y in range(yb):
        total = total + acc_ref[3, pl.ds(rows + y, c, stride=yb), :]
    place(27, jnp.where(lane == row * yb, total, 0.0))
    r = lax.broadcasted_iota(jnp.int32, (4 * rows, 4 * c), 0)
    s = lax.broadcasted_iota(jnp.int32, (4 * rows, 4 * c), 1)
    gather = jnp.where(r // yb == s, 1.0, 0.0).astype(F32)
    flat = jnp.dot(fold_ref[...], gather, preferred_element_type=F32, precision=lax.Precision.HIGHEST)
    size = parts.shape[1]
    for owner in range(n):
        lo, hi = owner * size, min((owner + 1) * size, 7 * c)
        if hi > lo:
            parts[owner, 0:hi - lo] = flat[lo:hi]
        if hi - lo < size:
            lo = max(hi - lo, 0)
            parts[owner, lo:size] = jnp.zeros((size - lo, 128), F32)
    each(lambda d, to, source: scatter(d, to).start())

    def inner_back(b):
        for x in range(1, nx - 1, 2):
            backward(b, x, 2)

    over_samples(inner_back)

    def outer_back(b):
        received_both(delta, b)
        shift_delta(b, 0)
        shift_delta(b, nx + 1)
        backward(b, 0, 1)
        backward(b, nx - 1, 1)
        result(1, b).start()

    outer_back(0)
    each(lambda d, to, source: scatter(d, to).wait_recv())
    own = (parts[me] + jnp.sum(received[...], axis=0)) * scale
    mine[...] = own
    gathered[me] = own
    each(lambda d, to, source: spread(d, me, to).start())
    for b in range(1, nb):
        outer_back(b)
    each(lambda d, to, source: spread(d, source, to).wait_recv())
    sums_ref[...] = gathered[...]
    for b in range(nb):
        sent_both(face, b)
        sent_both(delta, b)
        result(0, b).wait()
        result(1, b).wait()
    each(lambda d, to, source: scatter(d, to).wait_send())
    each(lambda d, to, source: spread(d, me, to).wait_send())


def chunk_rows(c, n):
    rows = 28 * c * c // 128
    return -(-rows // (8 * n)) * 8


def main(activations, cotangent, taps, channel_bias, n, scale):
    nb, c, nx, yb, z = activations.shape
    rows = c * yb
    size = chunk_rows(c, n)
    hbm = pl.BlockSpec(memory_space=pl.ANY)
    vmem = pl.BlockSpec(memory_space=pltpu.VMEM)
    dma = pltpu.SemaphoreType.DMA
    block = jax.ShapeDtypeStruct((nb, c, nx, yb, z), BF16)
    return pl.pallas_call(
        functools.partial(main_kernel, n=n, scale=scale),
        in_specs=[hbm, hbm, vmem, vmem],
        out_specs=[hbm, hbm, vmem],
        out_shape=[block, block, jax.ShapeDtypeStruct((n, size, 128), F32)],
        scratch_shapes=[
            pltpu.VMEM((nb, c, nx, yb, z), BF16),
            pltpu.VMEM((nb, c, nx, yb, z), BF16),
            pltpu.VMEM((2, nb, c, yb, z), BF16),
            pltpu.VMEM((nb, (nx + 2) * 3 * rows, z), BF16),
            pltpu.VMEM((nb, (nx + 2) * 3 * rows, z), BF16),
            pltpu.VMEM((nb, c, nx, yb, z), BF16),
            pltpu.VMEM((nb, c, nx, yb, z), BF16),
            pltpu.VMEM((2 * rows, 12 * rows), BF16),
            pltpu.VMEM((2 * rows, 12 * rows), BF16),
            pltpu.VMEM((4, 3 * rows, rows), F32),
            pltpu.VMEM((7 * c, 4 * rows), F32),
            pltpu.VMEM((n, size, 128), F32),
            pltpu.VMEM((n - 1, size, 128), F32),
            pltpu.VMEM((size, 128), F32),
            pltpu.VMEM((n, size, 128), F32),
            dma((2, nb)), dma((2, nb)), dma((2, nb)), dma((2, nb)), dma((2, nb)), dma((2, nb)),
            dma((n - 1,)), dma((n - 1,)), dma((n - 1,)), dma((n - 1,)),
        ],
        compiler_params=pltpu.CompilerParams(
            collective_id=0, has_side_effects=True, vmem_limit_bytes=52 * 1024 * 1024),
        cost_estimate=pl.CostEstimate(flops=10 << 30, bytes_accessed=10 << 20, transcendentals=0),
        name="conv",
    )(activations, cotangent, taps, channel_bias.reshape(1, c))


def finish_kernel(activated_ref, grad_ref, sums_ref, activated_out, grad_out, kernel_out, bias_out, sem):
    nb = activated_ref.shape[0]
    c = bias_out.shape[1]
    copies = []
    for b in range(nb):
        copies.append(pltpu.make_async_copy(activated_ref.at[b], activated_out.at[b], sem.at[0, b]))
        copies.append(pltpu.make_async_copy(grad_ref.at[b], grad_out.at[b], sem.at[1, b]))
    for copy in copies:
        copy.start()
    flat = sums_ref[...].reshape(-1, 128)
    for tap in range(27):
        row, col = tap // 4 * c, tap % 4 * c
        kernel_out[tap] = flat[row:row + c, col:col + c]
    bias_out[...] = jnp.sum(flat[6 * c:7 * c, 3 * c:4 * c], axis=0, keepdims=True)
    for copy in copies:
        copy.wait()


def finish(activated, grad_input, sums):
    nb = activated.shape[0]
    c = activated.shape[1]
    hbm = pl.BlockSpec(memory_space=pl.ANY)
    vmem = pl.BlockSpec(memory_space=pltpu.VMEM)
    block = jax.ShapeDtypeStruct(activated.shape, BF16)
    return pl.pallas_call(
        finish_kernel,
        in_specs=[hbm, hbm, vmem],
        out_specs=[hbm, hbm, vmem, vmem],
        out_shape=[block, block, jax.ShapeDtypeStruct((27, c, c), F32), jax.ShapeDtypeStruct((1, c), F32)],
        scratch_shapes=[pltpu.SemaphoreType.DMA((2, nb))],
        cost_estimate=pl.CostEstimate(flops=1 << 20, bytes_accessed=8 << 20, transcendentals=0),
        name="finish",
    )(activated, grad_input, sums)


def per_device(activations, cotangent, kernel, channel_bias):
    nb, c, nx, yb, z = activations.shape
    n = lax.axis_size("gx")
    taps = jnp.transpose(kernel, (2, 3, 4, 0, 1)).reshape(27, c, c)
    cells = nb * nx * yb * z * n
    activated, grad_input, sums = main(activations, cotangent, taps, channel_bias, n, float(cells) ** -0.5)
    activated, grad_input, kernel_sums, bias_sums = finish(activated, grad_input, sums)
    grad_kernel = jnp.transpose(kernel_sums.reshape(3, 3, 3, c, c), (3, 4, 0, 1, 2))
    return activated, grad_input, grad_kernel, bias_sums.reshape(c)


def solution(mesh):
    placed = (P("grp", None, "gx", None, None), P("grp", None, "gx", None, None), P(), P())
    return jax.shard_map(
        per_device,
        mesh=mesh,
        in_specs=placed,
        out_specs=(
            P("grp", None, "gx", None, None),
            P("grp", None, "gx", None, None),
            P("grp", None, None, None, None),
            P("grp"),
        ),
        check_vma=False,
    )
```

```python
import functools

import jax
import jax.numpy as jnp
from jax import lax
from jax.experimental import pallas as pl
from jax.experimental.pallas import tpu as pltpu
from jax.sharding import PartitionSpec as P

F32 = jnp.float32
BF16 = jnp.bfloat16
MESH = pl.DeviceIdType.MESH
NT = (((1,), (1,)), ((), ()))
ZC = 256


def one_hot_rows(rows, group, dtype):
    r = lax.broadcasted_iota(jnp.int32, (rows, rows // group), 0)
    c = lax.broadcasted_iota(jnp.int32, (rows, rows // group), 1)
    return jnp.where(r // group == c, 1.0, 0.0).astype(dtype)


def one_hot_cols(rows, group, dtype):
    r = lax.broadcasted_iota(jnp.int32, (rows // group, rows), 0)
    c = lax.broadcasted_iota(jnp.int32, (rows // group, rows), 1)
    return jnp.where(c // group == r, 1.0, 0.0).astype(dtype)


def shifted(v):
    zero = jnp.zeros((v.shape[0], 1), v.dtype)
    return (
        jnp.concatenate([zero, v[:, :-1]], axis=1),
        jnp.concatenate([v[:, 1:], zero], axis=1),
    )


def build_weights(taps_ref, w_ref, w_back_ref, rows, yb):
    c = rows // yb
    spread_rows = one_hot_rows(rows, yb, BF16)
    spread_cols = one_hot_cols(rows, yb, BF16)
    r = lax.broadcasted_iota(jnp.int32, (rows, rows), 0)
    s = lax.broadcasted_iota(jnp.int32, (rows, rows), 1)
    offset = s % yb - r % yb
    wide = jnp.dot(taps_ref[...].reshape(27 * c, c), spread_cols, preferred_element_type=F32).astype(BF16)
    w_ref[...] = jnp.zeros_like(w_ref)
    w_back_ref[...] = jnp.zeros_like(w_back_ref)
    for i in range(3):
        for k in range(3):
            block = jnp.zeros((rows, rows), F32)
            for j in range(3):
                tap = (i * 3 + j) * 3 + k
                full = jnp.dot(spread_rows, wide[tap * c:(tap + 1) * c], preferred_element_type=F32)
                block = jnp.where(offset == j - 1, full, block)
            back = block.T.astype(BF16)
            block = block.astype(BF16)
            for xo in range(2):
                at = slice(xo * rows, (xo + 1) * rows)
                ahead = ((xo + i) * 3 + k) * rows
                behind = ((xo + 2 - i) * 3 + k) * rows
                w_ref[at, ahead:ahead + rows] = block
                w_back_ref[at, behind:behind + rows] = back


def main_kernel(act_ref, cot_ref, taps_ref, bias_ref, activated_ref, grad_ref, sums_ref,
                act_v, cot_v, halo, s_ref, d_ref, activated_v, grad_v, w_ref, w_back_ref,
                acc_ref, fold_ref, parts, received, mine, gathered,
                load_sem, face_send, face_recv, delta_send, delta_recv, out_sem,
                send1, recv1, send2, recv2, *, n, scale):
    nb, c, nx, yb, z = act_v.shape
    rows = c * yb
    me = lax.axis_index("gx")
    up, down = lax.rem(me + 1, n), lax.rem(me + n - 1, n)
    has_down, has_up = me > 0, me < n - 1

    def load(b):
        return (pltpu.make_async_copy(act_ref.at[b], act_v.at[b], load_sem.at[0, b]),
                pltpu.make_async_copy(cot_ref.at[b], cot_v.at[b], load_sem.at[1, b]))

    def face(side, b):
        return pltpu.make_async_remote_copy(
            src_ref=act_ref.at[b, :, nx - 1 if side == 0 else 0], dst_ref=halo.at[side, b],
            send_sem=face_send.at[side, b], recv_sem=face_recv.at[side, b],
            device_id={"gx": up if side == 0 else down}, device_id_type=MESH)

    def centre(slot):
        return pl.ds((slot * 3 + 1) * rows, rows)

    def delta(side, b):
        return pltpu.make_async_remote_copy(
            src_ref=d_ref.at[b, centre(nx if side == 0 else 1)],
            dst_ref=d_ref.at[b, centre(0 if side == 0 else nx + 1)],
            send_sem=delta_send.at[side, b], recv_sem=delta_recv.at[side, b],
            device_id={"gx": up if side == 0 else down}, device_id_type=MESH)

    def start_both(copy, b):
        @pl.when(has_up)
        def _():
            copy(0, b).start()

        @pl.when(has_down)
        def _():
            copy(1, b).start()

    def received_both(copy, b):
        @pl.when(has_down)
        def _():
            copy(0, b).wait_recv()

        @pl.when(has_up)
        def _():
            copy(1, b).wait_recv()

    def sent_both(copy, b):
        @pl.when(has_up)
        def _():
            copy(0, b).wait_send()

        @pl.when(has_down)
        def _():
            copy(1, b).wait_send()

    def result(which, b):
        src, dst = ((activated_v, activated_ref), (grad_v, grad_ref))[which]
        return pltpu.make_async_copy(src.at[b], dst.at[b], out_sem.at[which, b])

    def each(f):
        def step(d, carry):
            f(d, lax.rem(me + d, n), lax.rem(me + n - d, n))
            return carry
        lax.fori_loop(1, n, step, 0)

    def scatter(d, owner):
        return pltpu.make_async_remote_copy(
            src_ref=parts.at[owner], dst_ref=received.at[d - 1], send_sem=send1.at[d - 1], recv_sem=recv1.at[d - 1],
            device_id={"gx": owner}, device_id_type=MESH)

    def spread(d, slot, peer):
        return pltpu.make_async_remote_copy(
            src_ref=mine, dst_ref=gathered.at[slot], send_sem=send2.at[d - 1], recv_sem=recv2.at[d - 1],
            device_id={"gx": peer}, device_id_type=MESH)

    def over_samples(f):
        def step(b, carry):
            f(b)
            return carry
        lax.fori_loop(0, nb, step, 0)

    for b in range(nb):
        for copy in load(b):
            copy.start()
    barrier = pltpu.get_barrier_semaphore()
    each(lambda d, to, source: pl.semaphore_signal(barrier, inc=1, device_id={"gx": to}, device_id_type=MESH))
    pl.semaphore_wait(barrier, n - 1)
    for b in range(nb):
        start_both(face, b)

    @pl.when(me == 0)
    def _():
        for b in range(nb):
            halo[0, b] = jnp.zeros((c, yb, z), BF16)
            d_ref[b, centre(0)] = jnp.zeros((rows, z), BF16)

    @pl.when(me == n - 1)
    def _():
        for b in range(nb):
            halo[1, b] = jnp.zeros((c, yb, z), BF16)
            d_ref[b, centre(nx + 1)] = jnp.zeros((rows, z), BF16)

    build_weights(taps_ref, w_ref, w_back_ref, rows, yb)
    column = jnp.sum(one_hot_rows(rows, yb, F32) * bias_ref[...], axis=1, keepdims=True)

    def fill(b, slot, v):
        before, after = shifted(v)
        for k, part in enumerate((before, v, after)):
            s_ref[b, pl.ds((slot * 3 + k) * rows, rows)] = part

    def shift_delta(b, slot):
        before, after = shifted(d_ref[b, centre(slot)])
        d_ref[b, pl.ds(slot * 3 * rows, rows)] = after
        d_ref[b, pl.ds((slot * 3 + 2) * rows, rows)] = before

    def forward(b, x, width):
        depth = (width + 2) * 3 * rows
        for m in range(z // ZC):
            zs = slice(m * ZC, (m + 1) * ZC)
            pre = jnp.dot(w_ref[0:width * rows, 0:depth], s_ref[b, pl.ds(x * 3 * rows, depth), zs],
                          preferred_element_type=F32)
            for xo in range(width):
                t = pre[xo * rows:(xo + 1) * rows] + column
                cumulative = 0.5 * (1.0 + lax.erf(t * 0.7071067811865476))
                density = jnp.exp(-0.5 * t * t) * 0.3989422804014327
                activated_v[b, :, x + xo, :, zs] = (t * cumulative).astype(BF16).reshape(c, yb, ZC)
                g = cot_v[b, :, x + xo, :, zs].reshape(rows, ZC).astype(F32)
                d_ref[b, centre(x + xo + 1), zs] = (g * (cumulative + t * density)).astype(BF16)

    def backward(b, x, width):
        depth = (width + 2) * 3 * rows
        for m in range(z // ZC):
            zs = slice(m * ZC, (m + 1) * ZC)
            g = jnp.dot(w_back_ref[0:width * rows, 0:depth], d_ref[b, pl.ds(x * 3 * rows, depth), zs],
                        preferred_element_type=F32)
            for xo in range(width):
                part = g[xo * rows:(xo + 1) * rows].astype(BF16)
                grad_v[b, :, x + xo, :, zs] = part.reshape(c, yb, ZC)

    def inner(b):
        for copy in load(b):
            copy.wait()
        for x in range(nx):
            fill(b, x + 1, act_v[b, :, x].reshape(rows, z))
        for x in range(1, nx - 1, 2):
            forward(b, x, 2)
        for x in range(1, nx - 1):
            shift_delta(b, x + 1)

    over_samples(inner)
    acc_ref[...] = jnp.zeros_like(acc_ref)

    def outer(b):
        received_both(face, b)
        fill(b, 0, halo[0, b].reshape(rows, z))
        fill(b, nx + 1, halo[1, b].reshape(rows, z))
        forward(b, 0, 1)
        forward(b, nx - 1, 1)
        start_both(delta, b)
        result(0, b).start()
        shift_delta(b, 1)
        shift_delta(b, nx)
        for x in range(nx):
            planes = [s_ref[b, centre(x + i)] for i in range(3)]
            right = jnp.concatenate(planes + [jnp.ones((rows, z), BF16)], axis=0)
            product = lax.dot_general(d_ref[b, pl.ds((x + 1) * 3 * rows, 3 * rows)], right, NT,
                                      preferred_element_type=F32)
            for i in range(4):
                acc_ref[i] += product[:, i * rows:(i + 1) * rows]

    over_samples(outer)

    lane = lax.broadcasted_iota(jnp.int32, (c, rows), 1)
    row = lax.broadcasted_iota(jnp.int32, (c, rows), 0)

    def place(tap, value):
        at, col = tap // 4 * c, tap % 4 * rows
        fold_ref[at:at + c, col:col + rows] = value

    for i in range(3):
        for k in range(3):
            lines = [acc_ref[i, pl.ds(k * rows + y, c, stride=yb), :] for y in range(yb)]
            for j in range(3):
                value = jnp.zeros((c, rows), F32)
                for y in range(yb):
                    if 0 <= y + j - 1 < yb:
                        value = jnp.where(lane % yb == y + j - 1, lines[y], value)
                place((i * 3 + j) * 3 + k, value)
    total = jnp.zeros((c, rows), F32)
    for y in range(yb):
        total = total + acc_ref[3, pl.ds(rows + y, c, stride=yb), :]
    place(27, jnp.where(lane == row * yb, total, 0.0))
    r = lax.broadcasted_iota(jnp.int32, (4 * rows, 4 * c), 0)
    s = lax.broadcasted_iota(jnp.int32, (4 * rows, 4 * c), 1)
    gather = jnp.where(r // yb == s, 1.0, 0.0).astype(F32)
    flat = jnp.dot(fold_ref[...], gather, preferred_element_type=F32, precision=lax.Precision.HIGHEST)
    size = parts.shape[1]
    for owner in range(n):
        lo, hi = owner * size, min((owner + 1) * size, 7 * c)
        if hi > lo:
            parts[owner, 0:hi - lo] = flat[lo:hi]
        if hi - lo < size:
            lo = max(hi - lo, 0)
            parts[owner, lo:size] = jnp.zeros((size - lo, 128), F32)
    each(lambda d, to, source: scatter(d, to).start())

    def inner_back(b):
        for x in range(1, nx - 1, 2):
            backward(b, x, 2)

    over_samples(inner_back)

    def outer_back(b):
        received_both(delta, b)
        shift_delta(b, 0)
        shift_delta(b, nx + 1)
        backward(b, 0, 1)
        backward(b, nx - 1, 1)
        result(1, b).start()

    outer_back(0)
    each(lambda d, to, source: scatter(d, to).wait_recv())
    own = (parts[me] + jnp.sum(received[...], axis=0)) * scale
    mine[...] = own
    gathered[me] = own
    each(lambda d, to, source: spread(d, me, to).start())
    for b in range(1, nb):
        outer_back(b)
    each(lambda d, to, source: spread(d, source, to).wait_recv())
    sums_ref[...] = gathered[...]
    for b in range(nb):
        sent_both(face, b)
        sent_both(delta, b)
        result(0, b).wait()
        result(1, b).wait()
    each(lambda d, to, source: scatter(d, to).wait_send())
    each(lambda d, to, source: spread(d, me, to).wait_send())


def chunk_rows(c, n):
    rows = 28 * c * c // 128
    return -(-rows // (8 * n)) * 8


def main(activations, cotangent, taps, channel_bias, n, scale):
    nb, c, nx, yb, z = activations.shape
    rows = c * yb
    size = chunk_rows(c, n)
    hbm = pl.BlockSpec(memory_space=pl.ANY)
    vmem = pl.BlockSpec(memory_space=pltpu.VMEM)
    dma = pltpu.SemaphoreType.DMA
    block = jax.ShapeDtypeStruct((nb, c, nx, yb, z), BF16)
    return pl.pallas_call(
        functools.partial(main_kernel, n=n, scale=scale),
        in_specs=[hbm, hbm, vmem, vmem],
        out_specs=[hbm, hbm, vmem],
        out_shape=[block, block, jax.ShapeDtypeStruct((n, size, 128), F32)],
        scratch_shapes=[
            pltpu.VMEM((nb, c, nx, yb, z), BF16),
            pltpu.VMEM((nb, c, nx, yb, z), BF16),
            pltpu.VMEM((2, nb, c, yb, z), BF16),
            pltpu.VMEM((nb, (nx + 2) * 3 * rows, z), BF16),
            pltpu.VMEM((nb, (nx + 2) * 3 * rows, z), BF16),
            pltpu.VMEM((nb, c, nx, yb, z), BF16),
            pltpu.VMEM((nb, c, nx, yb, z), BF16),
            pltpu.VMEM((2 * rows, 12 * rows), BF16),
            pltpu.VMEM((2 * rows, 12 * rows), BF16),
            pltpu.VMEM((4, 3 * rows, rows), F32),
            pltpu.VMEM((7 * c, 4 * rows), F32),
            pltpu.VMEM((n, size, 128), F32),
            pltpu.VMEM((n - 1, size, 128), F32),
            pltpu.VMEM((size, 128), F32),
            pltpu.VMEM((n, size, 128), F32),
            dma((2, nb)), dma((2, nb)), dma((2, nb)), dma((2, nb)), dma((2, nb)), dma((2, nb)),
            dma((n - 1,)), dma((n - 1,)), dma((n - 1,)), dma((n - 1,)),
        ],
        compiler_params=pltpu.CompilerParams(
            collective_id=0, has_side_effects=True, vmem_limit_bytes=52 * 1024 * 1024),
        cost_estimate=pl.CostEstimate(flops=10 << 30, bytes_accessed=10 << 20, transcendentals=0),
        name="conv",
    )(activations, cotangent, taps, channel_bias.reshape(1, c))


def finish_kernel(activated_ref, grad_ref, sums_ref, activated_out, grad_out, kernel_out, bias_out,
                  activated_v, grad_v, in_sem, out_sem):
    nb = activated_ref.shape[0]
    c = bias_out.shape[1]
    arrays = ((activated_ref, activated_v, activated_out), (grad_ref, grad_v, grad_out))
    reads = [[pltpu.make_async_copy(src.at[b], held.at[b], in_sem.at[w, b]) for b in range(nb)]
             for w, (src, held, _) in enumerate(arrays)]
    writes = [[pltpu.make_async_copy(held.at[b], dst.at[b], out_sem.at[w, b]) for b in range(nb)]
              for w, (_, held, dst) in enumerate(arrays)]
    for group in reads:
        for copy in group:
            copy.start()
    flat = sums_ref[...].reshape(-1, 128)
    for tap in range(27):
        row, col = tap // 4 * c, tap % 4 * c
        kernel_out[tap] = flat[row:row + c, col:col + c]
    bias_out[...] = jnp.sum(flat[6 * c:7 * c, 3 * c:4 * c], axis=0, keepdims=True)
    for came, goes in zip(reads, writes):
        for first, second in zip(came, goes):
            first.wait()
            second.start()
    for group in writes:
        for copy in group:
            copy.wait()


def finish(activated, grad_input, sums):
    nb = activated.shape[0]
    c = activated.shape[1]
    hbm = pl.BlockSpec(memory_space=pl.ANY)
    vmem = pl.BlockSpec(memory_space=pltpu.VMEM)
    block = jax.ShapeDtypeStruct(activated.shape, BF16)
    return pl.pallas_call(
        finish_kernel,
        in_specs=[hbm, hbm, vmem],
        out_specs=[hbm, hbm, vmem, vmem],
        out_shape=[block, block, jax.ShapeDtypeStruct((27, c, c), F32), jax.ShapeDtypeStruct((1, c), F32)],
        scratch_shapes=[pltpu.VMEM(activated.shape, BF16), pltpu.VMEM(activated.shape, BF16),
                        pltpu.SemaphoreType.DMA((2, nb)), pltpu.SemaphoreType.DMA((2, nb))],
        compiler_params=pltpu.CompilerParams(vmem_limit_bytes=16 * 1024 * 1024),
        cost_estimate=pl.CostEstimate(flops=1 << 20, bytes_accessed=8 << 20, transcendentals=0),
        name="finish",
    )(activated, grad_input, sums)


def per_device(activations, cotangent, kernel, channel_bias):
    nb, c, nx, yb, z = activations.shape
    n = lax.axis_size("gx")
    taps = jnp.transpose(kernel, (2, 3, 4, 0, 1)).reshape(27, c, c)
    cells = nb * nx * yb * z * n
    activated, grad_input, sums = main(activations, cotangent, taps, channel_bias, n, float(cells) ** -0.5)
    activated, grad_input, kernel_sums, bias_sums = finish(activated, grad_input, sums)
    grad_kernel = jnp.transpose(kernel_sums.reshape(3, 3, 3, c, c), (3, 4, 0, 1, 2))
    return activated, grad_input, grad_kernel, bias_sums.reshape(c)


def solution(mesh):
    placed = (P("grp", None, "gx", None, None), P("grp", None, "gx", None, None), P(), P())
    return jax.shard_map(
        per_device,
        mesh=mesh,
        in_specs=placed,
        out_specs=(
            P("grp", None, "gx", None, None),
            P("grp", None, "gx", None, None),
            P("grp", None, None, None, None),
            P("grp"),
        ),
        check_vma=False,
    )
```

```python
import functools

import jax
import jax.numpy as jnp
from jax import lax
from jax.experimental import pallas as pl
from jax.experimental.pallas import tpu as pltpu
from jax.sharding import PartitionSpec as P

F32 = jnp.float32
BF16 = jnp.bfloat16
MESH = pl.DeviceIdType.MESH
NT = (((1,), (1,)), ((), ()))
ZC = 256


def one_hot_rows(rows, group, dtype):
    r = lax.broadcasted_iota(jnp.int32, (rows, rows // group), 0)
    c = lax.broadcasted_iota(jnp.int32, (rows, rows // group), 1)
    return jnp.where(r // group == c, 1.0, 0.0).astype(dtype)


def one_hot_cols(rows, group, dtype):
    r = lax.broadcasted_iota(jnp.int32, (rows // group, rows), 0)
    c = lax.broadcasted_iota(jnp.int32, (rows // group, rows), 1)
    return jnp.where(c // group == r, 1.0, 0.0).astype(dtype)


def shifted(v):
    zero = jnp.zeros((v.shape[0], 1), v.dtype)
    return (
        jnp.concatenate([zero, v[:, :-1]], axis=1),
        jnp.concatenate([v[:, 1:], zero], axis=1),
    )


def build_weights(taps_ref, w_ref, w_back_ref, rows, yb):
    c = rows // yb
    spread_rows = one_hot_rows(rows, yb, BF16)
    spread_cols = one_hot_cols(rows, yb, BF16)
    r = lax.broadcasted_iota(jnp.int32, (rows, rows), 0)
    s = lax.broadcasted_iota(jnp.int32, (rows, rows), 1)
    offset = s % yb - r % yb
    wide = jnp.dot(taps_ref[...].reshape(27 * c, c), spread_cols, preferred_element_type=F32).astype(BF16)
    w_ref[...] = jnp.zeros_like(w_ref)
    w_back_ref[...] = jnp.zeros_like(w_back_ref)
    for i in range(3):
        for k in range(3):
            block = jnp.zeros((rows, rows), F32)
            for j in range(3):
                tap = (i * 3 + j) * 3 + k
                full = jnp.dot(spread_rows, wide[tap * c:(tap + 1) * c], preferred_element_type=F32)
                block = jnp.where(offset == j - 1, full, block)
            back = block.T.astype(BF16)
            block = block.astype(BF16)
            for xo in range(2):
                at = slice(xo * rows, (xo + 1) * rows)
                ahead = ((xo + i) * 3 + k) * rows
                behind = ((xo + 2 - i) * 3 + k) * rows
                w_ref[at, ahead:ahead + rows] = block
                w_back_ref[at, behind:behind + rows] = back


def main_kernel(act_ref, cot_ref, taps_ref, bias_ref, activated_v, grad_v, sums_ref,
                act_v, cot_v, taps_v, bias_v, halo, s_ref, d_ref, w_ref, w_back_ref,
                acc_ref, fold_ref, parts, received, mine, gathered,
                load_sem, small_sem, face_send, face_recv, delta_send, delta_recv,
                send1, recv1, send2, recv2, *, n, scale):
    nb, c, nx, yb, z = act_v.shape
    rows = c * yb
    me = lax.axis_index("gx")
    up, down = lax.rem(me + 1, n), lax.rem(me + n - 1, n)
    has_down, has_up = me > 0, me < n - 1

    def load(b):
        return (pltpu.make_async_copy(act_ref.at[b], act_v.at[b], load_sem.at[0, b]),
                pltpu.make_async_copy(cot_ref.at[b], cot_v.at[b], load_sem.at[1, b]))

    def face(side, b):
        return pltpu.make_async_remote_copy(
            src_ref=act_ref.at[b, :, nx - 1 if side == 0 else 0], dst_ref=halo.at[side, b],
            send_sem=face_send.at[side, b], recv_sem=face_recv.at[side, b],
            device_id={"gx": up if side == 0 else down}, device_id_type=MESH)

    def centre(slot):
        return pl.ds((slot * 3 + 1) * rows, rows)

    def delta(side, b):
        return pltpu.make_async_remote_copy(
            src_ref=d_ref.at[b, centre(nx if side == 0 else 1)],
            dst_ref=d_ref.at[b, centre(0 if side == 0 else nx + 1)],
            send_sem=delta_send.at[side, b], recv_sem=delta_recv.at[side, b],
            device_id={"gx": up if side == 0 else down}, device_id_type=MESH)

    def start_both(copy, b):
        @pl.when(has_up)
        def _():
            copy(0, b).start()

        @pl.when(has_down)
        def _():
            copy(1, b).start()

    def received_both(copy, b):
        @pl.when(has_down)
        def _():
            copy(0, b).wait_recv()

        @pl.when(has_up)
        def _():
            copy(1, b).wait_recv()

    def sent_both(copy, b):
        @pl.when(has_up)
        def _():
            copy(0, b).wait_send()

        @pl.when(has_down)
        def _():
            copy(1, b).wait_send()

    small = (pltpu.make_async_copy(taps_ref, taps_v, small_sem.at[0]),
             pltpu.make_async_copy(bias_ref, bias_v, small_sem.at[1]))

    def each(f):
        def step(d, carry):
            f(d, lax.rem(me + d, n), lax.rem(me + n - d, n))
            return carry
        lax.fori_loop(1, n, step, 0)

    def scatter(d, owner):
        return pltpu.make_async_remote_copy(
            src_ref=parts.at[owner], dst_ref=received.at[d - 1], send_sem=send1.at[d - 1], recv_sem=recv1.at[d - 1],
            device_id={"gx": owner}, device_id_type=MESH)

    def spread(d, slot, peer):
        return pltpu.make_async_remote_copy(
            src_ref=mine, dst_ref=gathered.at[slot], send_sem=send2.at[d - 1], recv_sem=recv2.at[d - 1],
            device_id={"gx": peer}, device_id_type=MESH)

    def over_samples(f):
        def step(b, carry):
            f(b)
            return carry
        lax.fori_loop(0, nb, step, 0)

    for copy in small:
        copy.start()
    for b in range(nb):
        for copy in load(b):
            copy.start()
    barrier = pltpu.get_barrier_semaphore()
    each(lambda d, to, source: pl.semaphore_signal(barrier, inc=1, device_id={"gx": to}, device_id_type=MESH))
    pl.semaphore_wait(barrier, n - 1)
    for b in range(nb):
        start_both(face, b)

    @pl.when(me == 0)
    def _():
        for b in range(nb):
            halo[0, b] = jnp.zeros((c, yb, z), BF16)
            d_ref[b, centre(0)] = jnp.zeros((rows, z), BF16)

    @pl.when(me == n - 1)
    def _():
        for b in range(nb):
            halo[1, b] = jnp.zeros((c, yb, z), BF16)
            d_ref[b, centre(nx + 1)] = jnp.zeros((rows, z), BF16)

    for copy in small:
        copy.wait()
    build_weights(taps_v, w_ref, w_back_ref, rows, yb)
    column = jnp.sum(one_hot_rows(rows, yb, F32) * bias_v[...], axis=1, keepdims=True)

    def fill(b, slot, v):
        before, after = shifted(v)
        for k, part in enumerate((before, v, after)):
            s_ref[b, pl.ds((slot * 3 + k) * rows, rows)] = part

    def shift_delta(b, slot):
        before, after = shifted(d_ref[b, centre(slot)])
        d_ref[b, pl.ds(slot * 3 * rows, rows)] = after
        d_ref[b, pl.ds((slot * 3 + 2) * rows, rows)] = before

    def forward(b, x, width):
        depth = (width + 2) * 3 * rows
        for m in range(z // ZC):
            zs = slice(m * ZC, (m + 1) * ZC)
            pre = jnp.dot(w_ref[0:width * rows, 0:depth], s_ref[b, pl.ds(x * 3 * rows, depth), zs],
                          preferred_element_type=F32)
            for xo in range(width):
                t = pre[xo * rows:(xo + 1) * rows] + column
                cumulative = 0.5 * (1.0 + lax.erf(t * 0.7071067811865476))
                density = jnp.exp(-0.5 * t * t) * 0.3989422804014327
                activated_v[b, :, x + xo, :, zs] = (t * cumulative).astype(BF16).reshape(c, yb, ZC)
                g = cot_v[b, :, x + xo, :, zs].reshape(rows, ZC).astype(F32)
                d_ref[b, centre(x + xo + 1), zs] = (g * (cumulative + t * density)).astype(BF16)

    def backward(b, x, width):
        depth = (width + 2) * 3 * rows
        for m in range(z // ZC):
            zs = slice(m * ZC, (m + 1) * ZC)
            g = jnp.dot(w_back_ref[0:width * rows, 0:depth], d_ref[b, pl.ds(x * 3 * rows, depth), zs],
                        preferred_element_type=F32)
            for xo in range(width):
                part = g[xo * rows:(xo + 1) * rows].astype(BF16)
                grad_v[b, :, x + xo, :, zs] = part.reshape(c, yb, ZC)

    def inner(b):
        for copy in load(b):
            copy.wait()
        for x in range(nx):
            fill(b, x + 1, act_v[b, :, x].reshape(rows, z))
        for x in range(1, nx - 1, 2):
            forward(b, x, 2)
        for x in range(1, nx - 1):
            shift_delta(b, x + 1)

    over_samples(inner)
    acc_ref[...] = jnp.zeros_like(acc_ref)

    def outer(b):
        received_both(face, b)
        fill(b, 0, halo[0, b].reshape(rows, z))
        fill(b, nx + 1, halo[1, b].reshape(rows, z))
        forward(b, 0, 1)
        forward(b, nx - 1, 1)
        start_both(delta, b)
        shift_delta(b, 1)
        shift_delta(b, nx)
        for x in range(nx):
            planes = [s_ref[b, centre(x + i)] for i in range(3)]
            right = jnp.concatenate(planes + [jnp.ones((rows, z), BF16)], axis=0)
            product = lax.dot_general(d_ref[b, pl.ds((x + 1) * 3 * rows, 3 * rows)], right, NT,
                                      preferred_element_type=F32)
            for i in range(4):
                acc_ref[i] += product[:, i * rows:(i + 1) * rows]

    over_samples(outer)

    lane = lax.broadcasted_iota(jnp.int32, (c, rows), 1)
    row = lax.broadcasted_iota(jnp.int32, (c, rows), 0)

    def place(tap, value):
        at, col = tap // 4 * c, tap % 4 * rows
        fold_ref[at:at + c, col:col + rows] = value

    for i in range(3):
        for k in range(3):
            lines = [acc_ref[i, pl.ds(k * rows + y, c, stride=yb), :] for y in range(yb)]
            for j in range(3):
                value = jnp.zeros((c, rows), F32)
                for y in range(yb):
                    if 0 <= y + j - 1 < yb:
                        value = jnp.where(lane % yb == y + j - 1, lines[y], value)
                place((i * 3 + j) * 3 + k, value)
    total = jnp.zeros((c, rows), F32)
    for y in range(yb):
        total = total + acc_ref[3, pl.ds(rows + y, c, stride=yb), :]
    place(27, jnp.where(lane == row * yb, total, 0.0))
    r = lax.broadcasted_iota(jnp.int32, (4 * rows, 4 * c), 0)
    s = lax.broadcasted_iota(jnp.int32, (4 * rows, 4 * c), 1)
    gather = jnp.where(r // yb == s, 1.0, 0.0).astype(F32)
    flat = jnp.dot(fold_ref[...], gather, preferred_element_type=F32, precision=lax.Precision.HIGHEST)
    size = parts.shape[1]
    for owner in range(n):
        lo, hi = owner * size, min((owner + 1) * size, 7 * c)
        if hi > lo:
            parts[owner, 0:hi - lo] = flat[lo:hi]
        if hi - lo < size:
            lo = max(hi - lo, 0)
            parts[owner, lo:size] = jnp.zeros((size - lo, 128), F32)
    each(lambda d, to, source: scatter(d, to).start())

    def inner_back(b):
        for x in range(1, nx - 1, 2):
            backward(b, x, 2)

    over_samples(inner_back)

    def outer_back(b):
        received_both(delta, b)
        shift_delta(b, 0)
        shift_delta(b, nx + 1)
        backward(b, 0, 1)
        backward(b, nx - 1, 1)

    outer_back(0)
    each(lambda d, to, source: scatter(d, to).wait_recv())
    own = (parts[me] + jnp.sum(received[...], axis=0)) * scale
    mine[...] = own
    gathered[me] = own
    each(lambda d, to, source: spread(d, me, to).start())
    for b in range(1, nb):
        outer_back(b)
    each(lambda d, to, source: spread(d, source, to).wait_recv())
    sums_ref[...] = gathered[...]
    for b in range(nb):
        sent_both(face, b)
        sent_both(delta, b)
    each(lambda d, to, source: scatter(d, to).wait_send())
    each(lambda d, to, source: spread(d, me, to).wait_send())


def chunk_rows(c, n):
    rows = 28 * c * c // 128
    return -(-rows // (8 * n)) * 8


def main(activations, cotangent, taps, channel_bias, n, scale):
    nb, c, nx, yb, z = activations.shape
    rows = c * yb
    size = chunk_rows(c, n)
    hbm = pl.BlockSpec(memory_space=pltpu.HBM)
    vmem = pl.BlockSpec(memory_space=pltpu.VMEM)
    dma = pltpu.SemaphoreType.DMA
    block = jax.ShapeDtypeStruct((nb, c, nx, yb, z), BF16)
    return pl.pallas_call(
        functools.partial(main_kernel, n=n, scale=scale),
        in_specs=[hbm, hbm, hbm, hbm],
        out_specs=[vmem, vmem, vmem],
        out_shape=[block, block, jax.ShapeDtypeStruct((n, size, 128), F32)],
        scratch_shapes=[
            pltpu.VMEM((nb, c, nx, yb, z), BF16),
            pltpu.VMEM((nb, c, nx, yb, z), BF16),
            pltpu.VMEM(taps.shape, BF16),
            pltpu.VMEM((1, c), F32),
            pltpu.VMEM((2, nb, c, yb, z), BF16),
            pltpu.VMEM((nb, (nx + 2) * 3 * rows, z), BF16),
            pltpu.VMEM((nb, (nx + 2) * 3 * rows, z), BF16),
            pltpu.VMEM((2 * rows, 12 * rows), BF16),
            pltpu.VMEM((2 * rows, 12 * rows), BF16),
            pltpu.VMEM((4, 3 * rows, rows), F32),
            pltpu.VMEM((7 * c, 4 * rows), F32),
            pltpu.VMEM((n, size, 128), F32),
            pltpu.VMEM((n - 1, size, 128), F32),
            pltpu.VMEM((size, 128), F32),
            pltpu.VMEM((n, size, 128), F32),
            dma((2, nb)), dma((2,)), dma((2, nb)), dma((2, nb)), dma((2, nb)), dma((2, nb)),
            dma((n - 1,)), dma((n - 1,)), dma((n - 1,)), dma((n - 1,)),
        ],
        compiler_params=pltpu.CompilerParams(
            collective_id=0, has_side_effects=True, vmem_limit_bytes=49 * 1024 * 1024),
        cost_estimate=pl.CostEstimate(flops=10 << 30, bytes_accessed=10 << 20, transcendentals=0),
        name="conv",
    )(activations, cotangent, taps, channel_bias.reshape(1, c))


def finish_kernel(activated_ref, grad_ref, sums_ref, activated_out, grad_out, kernel_out, bias_out, sem):
    nb = activated_ref.shape[0]
    c = bias_out.shape[1]
    copies = [pltpu.make_async_copy(src.at[b], dst.at[b], sem.at[w, b])
              for w, (src, dst) in enumerate(((activated_ref, activated_out), (grad_ref, grad_out)))
              for b in range(nb)]
    for copy in copies:
        copy.start()
    flat = sums_ref[...].reshape(-1, 128)
    for tap in range(27):
        row, col = tap // 4 * c, tap % 4 * c
        kernel_out[tap] = flat[row:row + c, col:col + c]
    bias_out[...] = jnp.sum(flat[6 * c:7 * c, 3 * c:4 * c], axis=0, keepdims=True)
    for copy in copies:
        copy.wait()


def finish(activated, grad_input, sums):
    nb = activated.shape[0]
    c = activated.shape[1]
    hbm = pl.BlockSpec(memory_space=pl.ANY)
    vmem = pl.BlockSpec(memory_space=pltpu.VMEM)
    block = jax.ShapeDtypeStruct(activated.shape, BF16)
    return pl.pallas_call(
        finish_kernel,
        in_specs=[vmem, vmem, vmem],
        out_specs=[hbm, hbm, vmem, vmem],
        out_shape=[block, block, jax.ShapeDtypeStruct((27, c, c), F32), jax.ShapeDtypeStruct((1, c), F32)],
        scratch_shapes=[pltpu.SemaphoreType.DMA((2, nb))],
        compiler_params=pltpu.CompilerParams(vmem_limit_bytes=16 * 1024 * 1024),
        cost_estimate=pl.CostEstimate(flops=1 << 20, bytes_accessed=8 << 20, transcendentals=0),
        name="finish",
    )(activated, grad_input, sums)


def per_device(activations, cotangent, kernel, channel_bias):
    nb, c, nx, yb, z = activations.shape
    n = lax.axis_size("gx")
    taps = jnp.transpose(kernel, (2, 3, 4, 0, 1)).reshape(27, c, c)
    cells = nb * nx * yb * z * n
    activated, grad_input, sums = main(activations, cotangent, taps, channel_bias, n, float(cells) ** -0.5)
    activated, grad_input, kernel_sums, bias_sums = finish(activated, grad_input, sums)
    grad_kernel = jnp.transpose(kernel_sums.reshape(3, 3, 3, c, c), (3, 4, 0, 1, 2))
    return activated, grad_input, grad_kernel, bias_sums.reshape(c)


def solution(mesh):
    placed = (P("grp", None, "gx", None, None), P("grp", None, "gx", None, None), P(), P())
    return jax.shard_map(
        per_device,
        mesh=mesh,
        in_specs=placed,
        out_specs=(
            P("grp", None, "gx", None, None),
            P("grp", None, "gx", None, None),
            P("grp", None, None, None, None),
            P("grp"),
        ),
        check_vma=False,
    )
```

```python
import functools

import jax
import jax.numpy as jnp
from jax import lax
from jax.experimental import pallas as pl
from jax.experimental.pallas import tpu as pltpu
from jax.sharding import PartitionSpec as P

F32 = jnp.float32
BF16 = jnp.bfloat16
MESH = pl.DeviceIdType.MESH
NT = (((1,), (1,)), ((), ()))
ZC = 256
PIECES = 4


def one_hot_rows(rows, group, dtype):
    r = lax.broadcasted_iota(jnp.int32, (rows, rows // group), 0)
    c = lax.broadcasted_iota(jnp.int32, (rows, rows // group), 1)
    return jnp.where(r // group == c, 1.0, 0.0).astype(dtype)


def one_hot_cols(rows, group, dtype):
    r = lax.broadcasted_iota(jnp.int32, (rows // group, rows), 0)
    c = lax.broadcasted_iota(jnp.int32, (rows // group, rows), 1)
    return jnp.where(c // group == r, 1.0, 0.0).astype(dtype)


def shifted(v):
    zero = jnp.zeros((v.shape[0], 1), v.dtype)
    return (
        jnp.concatenate([zero, v[:, :-1]], axis=1),
        jnp.concatenate([v[:, 1:], zero], axis=1),
    )


def build_weights(taps_ref, w_ref, w_back_ref, rows, yb):
    c = rows // yb
    spread_rows = one_hot_rows(rows, yb, BF16)
    spread_cols = one_hot_cols(rows, yb, BF16)
    r = lax.broadcasted_iota(jnp.int32, (rows, rows), 0)
    s = lax.broadcasted_iota(jnp.int32, (rows, rows), 1)
    offset = s % yb - r % yb
    wide = jnp.dot(taps_ref[...].reshape(27 * c, c), spread_cols, preferred_element_type=F32).astype(BF16)
    w_ref[...] = jnp.zeros_like(w_ref)
    w_back_ref[...] = jnp.zeros_like(w_back_ref)
    for i in range(3):
        for k in range(3):
            block = jnp.zeros((rows, rows), F32)
            for j in range(3):
                tap = (i * 3 + j) * 3 + k
                full = jnp.dot(spread_rows, wide[tap * c:(tap + 1) * c], preferred_element_type=F32)
                block = jnp.where(offset == j - 1, full, block)
            back = block.T.astype(BF16)
            block = block.astype(BF16)
            for xo in range(2):
                at = slice(xo * rows, (xo + 1) * rows)
                ahead = ((xo + i) * 3 + k) * rows
                behind = ((xo + 2 - i) * 3 + k) * rows
                w_ref[at, ahead:ahead + rows] = block
                w_back_ref[at, behind:behind + rows] = back


def main_kernel(act_ref, cot_ref, taps_ref, bias_ref, activated_v, grad_v, sums_ref,
                act_v, cot_v, taps_v, bias_v, halo, s_ref, d_ref, w_ref, w_back_ref,
                acc_ref, fold_ref, parts, pair, half, received, mine, gathered,
                load_sem, small_sem, face_send, face_recv, delta_send, delta_recv,
                pair_sem, send1, recv1, send2, recv2, *, n, scale):
    nb, c, nx, yb, z = act_v.shape
    rows = c * yb
    me = lax.axis_index("gx")
    up, down = lax.rem(me + 1, n), lax.rem(me + n - 1, n)
    has_down, has_up = me > 0, me < n - 1

    def load(b):
        return (pltpu.make_async_copy(act_ref.at[b], act_v.at[b], load_sem.at[0, b]),
                pltpu.make_async_copy(cot_ref.at[b], cot_v.at[b], load_sem.at[1, b]))

    def face(side, b):
        return pltpu.make_async_remote_copy(
            src_ref=act_ref.at[b, :, nx - 1 if side == 0 else 0], dst_ref=halo.at[side, b],
            send_sem=face_send.at[side, b], recv_sem=face_recv.at[side, b],
            device_id={"gx": up if side == 0 else down}, device_id_type=MESH)

    def centre(slot):
        return pl.ds((slot * 3 + 1) * rows, rows)

    def delta(side, b):
        return pltpu.make_async_remote_copy(
            src_ref=d_ref.at[b, centre(nx if side == 0 else 1)],
            dst_ref=d_ref.at[b, centre(0 if side == 0 else nx + 1)],
            send_sem=delta_send.at[side, b], recv_sem=delta_recv.at[side, b],
            device_id={"gx": up if side == 0 else down}, device_id_type=MESH)

    def start_both(copy, b):
        @pl.when(has_up)
        def _():
            copy(0, b).start()

        @pl.when(has_down)
        def _():
            copy(1, b).start()

    def received_both(copy, b):
        @pl.when(has_down)
        def _():
            copy(0, b).wait_recv()

        @pl.when(has_up)
        def _():
            copy(1, b).wait_recv()

    def sent_both(copy, b):
        @pl.when(has_up)
        def _():
            copy(0, b).wait_send()

        @pl.when(has_down)
        def _():
            copy(1, b).wait_send()

    small = (pltpu.make_async_copy(taps_ref, taps_v, small_sem.at[0]),
             pltpu.make_async_copy(bias_ref, bias_v, small_sem.at[1]))

    def each(f):
        def step(d, carry):
            f(d, lax.rem(me + d, n), lax.rem(me + n - d, n))
            return carry
        lax.fori_loop(1, n, step, 0)

    core, chip, chips = lax.rem(me, 2), lax.div(me, 2), n // 2

    def each_chip(f):
        def step(d, carry):
            f(d, lax.rem(chip + d, chips), lax.rem(chip + chips - d, chips))
            return carry
        lax.fori_loop(1, chips, step, 0)

    def exchange():
        return pltpu.make_async_remote_copy(
            src_ref=parts.at[1 - core], dst_ref=pair, send_sem=pair_sem.at[0], recv_sem=pair_sem.at[1],
            device_id={"gx": me + 1 - 2 * core}, device_id_type=MESH)

    def scatter(d, owner):
        return pltpu.make_async_remote_copy(
            src_ref=half.at[owner], dst_ref=received.at[d - 1], send_sem=send1.at[d - 1], recv_sem=recv1.at[d - 1],
            device_id={"gx": 2 * owner + core}, device_id_type=MESH)

    def slot(device):
        return lax.rem(device, 2) * chips + lax.div(device, 2)

    def spread(d, source, peer):
        return pltpu.make_async_remote_copy(
            src_ref=mine, dst_ref=gathered.at[slot(source)], send_sem=send2.at[d - 1], recv_sem=recv2.at[d - 1],
            device_id={"gx": peer}, device_id_type=MESH)

    def over_samples(f):
        def step(b, carry):
            f(b)
            return carry
        lax.fori_loop(0, nb, step, 0)

    for copy in small:
        copy.start()
    for b in range(nb):
        for copy in load(b):
            copy.start()
    barrier = pltpu.get_barrier_semaphore()
    each(lambda d, to, source: pl.semaphore_signal(barrier, inc=1, device_id={"gx": to}, device_id_type=MESH))
    pl.semaphore_wait(barrier, n - 1)
    for b in range(nb):
        start_both(face, b)

    @pl.when(me == 0)
    def _():
        for b in range(nb):
            halo[0, b] = jnp.zeros((c, yb, z), BF16)
            d_ref[b, centre(0)] = jnp.zeros((rows, z), BF16)

    @pl.when(me == n - 1)
    def _():
        for b in range(nb):
            halo[1, b] = jnp.zeros((c, yb, z), BF16)
            d_ref[b, centre(nx + 1)] = jnp.zeros((rows, z), BF16)

    for copy in small:
        copy.wait()
    build_weights(taps_v, w_ref, w_back_ref, rows, yb)
    column = jnp.sum(one_hot_rows(rows, yb, F32) * bias_v[...], axis=1, keepdims=True)

    def fill(b, slot, v):
        before, after = shifted(v)
        for k, part in enumerate((before, v, after)):
            s_ref[b, pl.ds((slot * 3 + k) * rows, rows)] = part

    def shift_delta(b, slot):
        before, after = shifted(d_ref[b, centre(slot)])
        d_ref[b, pl.ds(slot * 3 * rows, rows)] = after
        d_ref[b, pl.ds((slot * 3 + 2) * rows, rows)] = before

    def forward(b, x, width):
        depth = (width + 2) * 3 * rows
        for m in range(z // ZC):
            zs = slice(m * ZC, (m + 1) * ZC)
            pre = jnp.dot(w_ref[0:width * rows, 0:depth], s_ref[b, pl.ds(x * 3 * rows, depth), zs],
                          preferred_element_type=F32)
            for xo in range(width):
                t = pre[xo * rows:(xo + 1) * rows] + column
                cumulative = 0.5 * (1.0 + lax.erf(t * 0.7071067811865476))
                density = jnp.exp(-0.5 * t * t) * 0.3989422804014327
                activated_v[b, :, x + xo, :, zs] = (t * cumulative).astype(BF16).reshape(c, yb, ZC)
                g = cot_v[b, :, x + xo, :, zs].reshape(rows, ZC).astype(F32)
                d_ref[b, centre(x + xo + 1), zs] = (g * (cumulative + t * density)).astype(BF16)

    def backward(b, x, width):
        depth = (width + 2) * 3 * rows
        for m in range(z // ZC):
            zs = slice(m * ZC, (m + 1) * ZC)
            g = jnp.dot(w_back_ref[0:width * rows, 0:depth], d_ref[b, pl.ds(x * 3 * rows, depth), zs],
                        preferred_element_type=F32)
            for xo in range(width):
                part = g[xo * rows:(xo + 1) * rows].astype(BF16)
                grad_v[b, :, x + xo, :, zs] = part.reshape(c, yb, ZC)

    def inner(b):
        for copy in load(b):
            copy.wait()
        for x in range(nx):
            fill(b, x + 1, act_v[b, :, x].reshape(rows, z))
        for x in range(1, nx - 1, 2):
            forward(b, x, 2)
        for x in range(1, nx - 1):
            shift_delta(b, x + 1)

    over_samples(inner)
    acc_ref[...] = jnp.zeros_like(acc_ref)

    def outer(b):
        received_both(face, b)
        fill(b, 0, halo[0, b].reshape(rows, z))
        fill(b, nx + 1, halo[1, b].reshape(rows, z))
        forward(b, 0, 1)
        forward(b, nx - 1, 1)
        @pl.when(b < nb - 1)
        def _():
            start_both(delta, b)

        shift_delta(b, 1)
        shift_delta(b, nx)
        for x in range(nx):
            planes = [s_ref[b, centre(x + i)] for i in range(3)]
            right = jnp.concatenate(planes + [jnp.ones((rows, z), BF16)], axis=0)
            product = lax.dot_general(d_ref[b, pl.ds((x + 1) * 3 * rows, 3 * rows)], right, NT,
                                      preferred_element_type=F32)
            for i in range(4):
                acc_ref[i] += product[:, i * rows:(i + 1) * rows]

    over_samples(outer)

    lane = lax.broadcasted_iota(jnp.int32, (c, rows), 1)
    row = lax.broadcasted_iota(jnp.int32, (c, rows), 0)

    def place(tap, value):
        at, col = tap // 4 * c, tap % 4 * rows
        fold_ref[at:at + c, col:col + rows] = value

    for i in range(3):
        for k in range(3):
            lines = [acc_ref[i, pl.ds(k * rows + y, c, stride=yb), :] for y in range(yb)]
            for j in range(3):
                value = jnp.zeros((c, rows), F32)
                for y in range(yb):
                    if 0 <= y + j - 1 < yb:
                        value = jnp.where(lane % yb == y + j - 1, lines[y], value)
                place((i * 3 + j) * 3 + k, value)
    total = jnp.zeros((c, rows), F32)
    for y in range(yb):
        total = total + acc_ref[3, pl.ds(rows + y, c, stride=yb), :]
    place(27, jnp.where(lane == row * yb, total, 0.0))
    r = lax.broadcasted_iota(jnp.int32, (4 * rows, 4 * c), 0)
    s = lax.broadcasted_iota(jnp.int32, (4 * rows, 4 * c), 1)
    gather = jnp.where(r // yb == s, 1.0, 0.0).astype(F32)
    flat = jnp.dot(fold_ref[...], gather, preferred_element_type=F32, precision=lax.Precision.HIGHEST)
    size = parts.shape[2]
    for at in range(n):
        lo, hi = at * size, min((at + 1) * size, 7 * c)
        filled = max(hi - lo, 0)
        if filled:
            parts[at // chips, at % chips, 0:filled] = flat[lo:hi]
        if filled < size:
            parts[at // chips, at % chips, filled:size] = jnp.zeros((size - filled, 128), F32)
    exchange().start()

    def inner_back(b):
        for x in range(1, nx - 1, 2):
            backward(b, x, 2)

    exchange().wait_recv()
    half[...] = parts[core] + pair[...]
    each_chip(lambda d, to, source: scatter(d, to).start())
    start_both(delta, nb - 1)
    over_samples(inner_back)

    def outer_back(b):
        received_both(delta, b)
        shift_delta(b, 0)
        shift_delta(b, nx + 1)
        backward(b, 0, 1)
        backward(b, nx - 1, 1)

    outer_back(0)
    each_chip(lambda d, to, source: scatter(d, to).wait_recv())
    mine[...] = ((half[chip] + jnp.sum(received[...], axis=0)) * scale).astype(BF16)
    each(lambda d, to, source: spread(d, me, to).start())
    gathered[slot(me)] = mine[...]
    for b in range(1, nb):
        outer_back(b)
    each(lambda d, to, source: spread(d, source, to).wait_recv())
    sums_ref[...] = gathered[...].astype(F32)
    for b in range(nb):
        sent_both(face, b)
        sent_both(delta, b)
    exchange().wait_send()
    each_chip(lambda d, to, source: scatter(d, to).wait_send())
    each(lambda d, to, source: spread(d, me, to).wait_send())


def chunk_rows(c, n):
    rows = 28 * c * c // 128
    return -(-rows // (16 * n)) * 16


def main(activations, cotangent, taps, channel_bias, n, scale):
    nb, c, nx, yb, z = activations.shape
    rows = c * yb
    size = chunk_rows(c, n)
    hbm = pl.BlockSpec(memory_space=pltpu.HBM)
    vmem = pl.BlockSpec(memory_space=pltpu.VMEM)
    dma = pltpu.SemaphoreType.DMA
    block = jax.ShapeDtypeStruct((nb, c, nx, yb, z), BF16)
    return pl.pallas_call(
        functools.partial(main_kernel, n=n, scale=scale),
        in_specs=[hbm, hbm, hbm, hbm],
        out_specs=[vmem, vmem, vmem],
        out_shape=[block, block, jax.ShapeDtypeStruct((n, size, 128), F32)],
        scratch_shapes=[
            pltpu.VMEM((nb, c, nx, yb, z), BF16),
            pltpu.VMEM((nb, c, nx, yb, z), BF16),
            pltpu.VMEM(taps.shape, BF16),
            pltpu.VMEM((1, c), F32),
            pltpu.VMEM((2, nb, c, yb, z), BF16),
            pltpu.VMEM((nb, (nx + 2) * 3 * rows, z), BF16),
            pltpu.VMEM((nb, (nx + 2) * 3 * rows, z), BF16),
            pltpu.VMEM((2 * rows, 12 * rows), BF16),
            pltpu.VMEM((2 * rows, 12 * rows), BF16),
            pltpu.VMEM((4, 3 * rows, rows), F32),
            pltpu.VMEM((7 * c, 4 * rows), F32),
            pltpu.VMEM((2, n // 2, size, 128), F32),
            pltpu.VMEM((n // 2, size, 128), F32),
            pltpu.VMEM((n // 2, size, 128), F32),
            pltpu.VMEM((n // 2 - 1, size, 128), F32),
            pltpu.VMEM((size, 128), BF16),
            pltpu.VMEM((n, size, 128), BF16),
            dma((2, nb)), dma((2,)), dma((2, nb)), dma((2, nb)), dma((2, nb)), dma((2, nb)),
            dma((2,)), dma((n // 2 - 1,)), dma((n // 2 - 1,)), dma((n - 1,)), dma((n - 1,)),
        ],
        compiler_params=pltpu.CompilerParams(
            collective_id=0, has_side_effects=True, vmem_limit_bytes=49 * 1024 * 1024),
        cost_estimate=pl.CostEstimate(flops=10 << 30, bytes_accessed=10 << 20, transcendentals=0),
        name="conv",
    )(activations, cotangent, taps, channel_bias.reshape(1, c))


def finish_kernel(activated_ref, grad_ref, sums_ref, activated_out, grad_out, kernel_out, bias_out, sem):
    nb = activated_ref.shape[0]
    c = bias_out.shape[1]
    step = c // PIECES
    copies = [pltpu.make_async_copy(src.at[b, p * step:(p + 1) * step], dst.at[b, p * step:(p + 1) * step],
                                    sem.at[w, b, p])
              for b in range(nb) for p in range(PIECES)
              for w, (src, dst) in enumerate(((activated_ref, activated_out), (grad_ref, grad_out)))]
    for copy in copies:
        copy.start()
    flat = sums_ref[...].reshape(-1, 128)
    for tap in range(27):
        row, col = tap // 4 * c, tap % 4 * c
        kernel_out[tap] = flat[row:row + c, col:col + c]
    bias_out[...] = jnp.sum(flat[6 * c:7 * c, 3 * c:4 * c], axis=0, keepdims=True)
    for copy in copies:
        copy.wait()


def finish(activated, grad_input, sums):
    nb = activated.shape[0]
    c = activated.shape[1]
    hbm = pl.BlockSpec(memory_space=pl.ANY)
    vmem = pl.BlockSpec(memory_space=pltpu.VMEM)
    block = jax.ShapeDtypeStruct(activated.shape, BF16)
    return pl.pallas_call(
        finish_kernel,
        in_specs=[vmem, vmem, vmem],
        out_specs=[hbm, hbm, vmem, vmem],
        out_shape=[block, block, jax.ShapeDtypeStruct((27, c, c), F32), jax.ShapeDtypeStruct((1, c), F32)],
        scratch_shapes=[pltpu.SemaphoreType.DMA((2, nb, PIECES))],
        compiler_params=pltpu.CompilerParams(vmem_limit_bytes=16 * 1024 * 1024),
        cost_estimate=pl.CostEstimate(flops=1 << 20, bytes_accessed=8 << 20, transcendentals=0),
        name="finish",
    )(activated, grad_input, sums)


def per_device(activations, cotangent, kernel, channel_bias):
    nb, c, nx, yb, z = activations.shape
    n = lax.axis_size("gx")
    taps = jnp.transpose(kernel, (2, 3, 4, 0, 1)).reshape(27, c, c)
    cells = nb * nx * yb * z * n
    activated, grad_input, sums = main(activations, cotangent, taps, channel_bias, n, float(cells) ** -0.5)
    activated, grad_input, kernel_sums, bias_sums = finish(activated, grad_input, sums)
    grad_kernel = jnp.transpose(kernel_sums.reshape(3, 3, 3, c, c), (3, 4, 0, 1, 2))
    return activated, grad_input, grad_kernel, bias_sums.reshape(c)


def solution(mesh):
    placed = (P("grp", None, "gx", None, None), P("grp", None, "gx", None, None), P(), P())
    return jax.shard_map(
        per_device,
        mesh=mesh,
        in_specs=placed,
        out_specs=(
            P("grp", None, "gx", None, None),
            P("grp", None, "gx", None, None),
            P("grp", None, None, None, None),
            P("grp"),
        ),
        check_vma=False,
    )
```

```python
import functools

import jax
import jax.numpy as jnp
from jax import lax
from jax.experimental import pallas as pl
from jax.experimental.pallas import tpu as pltpu
from jax.sharding import PartitionSpec as P

F32 = jnp.float32
BF16 = jnp.bfloat16
MESH = pl.DeviceIdType.MESH
NT = (((1,), (1,)), ((), ()))
ZC = 256
PIECES = 4


def one_hot_rows(rows, group, dtype):
    r = lax.broadcasted_iota(jnp.int32, (rows, rows // group), 0)
    c = lax.broadcasted_iota(jnp.int32, (rows, rows // group), 1)
    return jnp.where(r // group == c, 1.0, 0.0).astype(dtype)


def one_hot_cols(rows, group, dtype):
    r = lax.broadcasted_iota(jnp.int32, (rows // group, rows), 0)
    c = lax.broadcasted_iota(jnp.int32, (rows // group, rows), 1)
    return jnp.where(c // group == r, 1.0, 0.0).astype(dtype)


def shifted(v):
    zero = jnp.zeros((v.shape[0], 1), v.dtype)
    return (
        jnp.concatenate([zero, v[:, :-1]], axis=1),
        jnp.concatenate([v[:, 1:], zero], axis=1),
    )


def build_weights(taps_ref, w_ref, w_back_ref, rows, yb):
    c = rows // yb
    spread_rows = one_hot_rows(rows, yb, BF16)
    spread_cols = one_hot_cols(rows, yb, BF16)
    r = lax.broadcasted_iota(jnp.int32, (rows, rows), 0)
    s = lax.broadcasted_iota(jnp.int32, (rows, rows), 1)
    offset = s % yb - r % yb
    wide = jnp.dot(taps_ref[...].reshape(27 * c, c), spread_cols, preferred_element_type=F32).astype(BF16)
    w_ref[...] = jnp.zeros_like(w_ref)
    w_back_ref[...] = jnp.zeros_like(w_back_ref)
    for i in range(3):
        for k in range(3):
            block = jnp.zeros((rows, rows), F32)
            for j in range(3):
                tap = (i * 3 + j) * 3 + k
                full = jnp.dot(spread_rows, wide[tap * c:(tap + 1) * c], preferred_element_type=F32)
                block = jnp.where(offset == j - 1, full, block)
            back = block.T.astype(BF16)
            block = block.astype(BF16)
            for xo in range(2):
                at = slice(xo * rows, (xo + 1) * rows)
                ahead = ((xo + i) * 3 + k) * rows
                behind = ((xo + 2 - i) * 3 + k) * rows
                w_ref[at, ahead:ahead + rows] = block
                w_back_ref[at, behind:behind + rows] = back


def main_kernel(act_ref, cot_ref, taps_ref, bias_ref, activated_v, grad_v, sums_ref,
                act_v, cot_v, taps_v, bias_v, halo, s_ref, d_ref, w_ref, w_back_ref,
                acc_ref, fold_ref, parts, pair, half, received, mine, gathered,
                load_sem, small_sem, face_send, face_recv, delta_send, delta_recv,
                pair_sem, send1, recv1, send2, recv2, *, n, scale):
    nb, c, nx, yb, z = act_v.shape
    rows = c * yb
    me = lax.axis_index("gx")
    up, down = lax.rem(me + 1, n), lax.rem(me + n - 1, n)
    has_down, has_up = me > 0, me < n - 1

    def load(b):
        return (pltpu.make_async_copy(act_ref.at[b], act_v.at[b], load_sem.at[0, b]),
                pltpu.make_async_copy(cot_ref.at[b], cot_v.at[b], load_sem.at[1, b]))

    def face(side, b):
        return pltpu.make_async_remote_copy(
            src_ref=act_ref.at[b, :, nx - 1 if side == 0 else 0], dst_ref=halo.at[side, b],
            send_sem=face_send.at[side, b], recv_sem=face_recv.at[side, b],
            device_id={"gx": up if side == 0 else down}, device_id_type=MESH)

    def centre(slot):
        return pl.ds((slot * 3 + 1) * rows, rows)

    def delta(side, b):
        return pltpu.make_async_remote_copy(
            src_ref=d_ref.at[b, centre(nx if side == 0 else 1)],
            dst_ref=d_ref.at[b, centre(0 if side == 0 else nx + 1)],
            send_sem=delta_send.at[side, b], recv_sem=delta_recv.at[side, b],
            device_id={"gx": up if side == 0 else down}, device_id_type=MESH)

    def start_both(copy, b):
        @pl.when(has_up)
        def _():
            copy(0, b).start()

        @pl.when(has_down)
        def _():
            copy(1, b).start()

    def received_both(copy, b):
        @pl.when(has_down)
        def _():
            copy(0, b).wait_recv()

        @pl.when(has_up)
        def _():
            copy(1, b).wait_recv()

    def sent_both(copy, b):
        @pl.when(has_up)
        def _():
            copy(0, b).wait_send()

        @pl.when(has_down)
        def _():
            copy(1, b).wait_send()

    small = (pltpu.make_async_copy(taps_ref, taps_v, small_sem.at[0]),
             pltpu.make_async_copy(bias_ref, bias_v, small_sem.at[1]))

    def each(f):
        def step(d, carry):
            f(d, lax.rem(me + d, n), lax.rem(me + n - d, n))
            return carry
        lax.fori_loop(1, n, step, 0)

    core, chip, chips = lax.rem(me, 2), lax.div(me, 2), n // 2

    def each_chip(f):
        def step(d, carry):
            f(d, lax.rem(chip + d, chips), lax.rem(chip + chips - d, chips))
            return carry
        lax.fori_loop(1, chips, step, 0)

    def exchange():
        return pltpu.make_async_remote_copy(
            src_ref=parts.at[1 - core], dst_ref=pair, send_sem=pair_sem.at[0], recv_sem=pair_sem.at[1],
            device_id={"gx": me + 1 - 2 * core}, device_id_type=MESH)

    def scatter(d, owner):
        return pltpu.make_async_remote_copy(
            src_ref=half.at[owner], dst_ref=received.at[d - 1], send_sem=send1.at[d - 1], recv_sem=recv1.at[d - 1],
            device_id={"gx": 2 * owner + core}, device_id_type=MESH)

    def slot(device):
        return lax.rem(device, 2) * chips + lax.div(device, 2)

    def spread(d, source, peer):
        return pltpu.make_async_remote_copy(
            src_ref=mine, dst_ref=gathered.at[slot(source)], send_sem=send2.at[d - 1], recv_sem=recv2.at[d - 1],
            device_id={"gx": peer}, device_id_type=MESH)

    def over_samples(f):
        def step(b, carry):
            f(b)
            return carry
        lax.fori_loop(0, nb, step, 0)

    for copy in small:
        copy.start()
    for b in range(nb):
        for copy in load(b):
            copy.start()
    barrier = pltpu.get_barrier_semaphore()
    each(lambda d, to, source: pl.semaphore_signal(barrier, inc=1, device_id={"gx": to}, device_id_type=MESH))
    pl.semaphore_wait(barrier, n - 1)
    for b in range(nb):
        start_both(face, b)

    @pl.when(me == 0)
    def _():
        for b in range(nb):
            halo[0, b] = jnp.zeros((c, yb, z), BF16)
            d_ref[b, centre(0)] = jnp.zeros((rows, z), BF16)

    @pl.when(me == n - 1)
    def _():
        for b in range(nb):
            halo[1, b] = jnp.zeros((c, yb, z), BF16)
            d_ref[b, centre(nx + 1)] = jnp.zeros((rows, z), BF16)

    for copy in small:
        copy.wait()
    build_weights(taps_v, w_ref, w_back_ref, rows, yb)
    column = jnp.sum(one_hot_rows(rows, yb, F32) * bias_v[...], axis=1, keepdims=True)

    def fill(b, slot, v):
        before, after = shifted(v)
        for k, part in enumerate((before, v, after)):
            s_ref[b, pl.ds((slot * 3 + k) * rows, rows)] = part

    def shift_delta(b, slot):
        before, after = shifted(d_ref[b, centre(slot)])
        d_ref[b, pl.ds(slot * 3 * rows, rows)] = after
        d_ref[b, pl.ds((slot * 3 + 2) * rows, rows)] = before

    def forward(b, x, width):
        depth = (width + 2) * 3 * rows
        for m in range(z // ZC):
            zs = slice(m * ZC, (m + 1) * ZC)
            pre = jnp.dot(w_ref[0:width * rows, 0:depth], s_ref[b, pl.ds(x * 3 * rows, depth), zs],
                          preferred_element_type=F32)
            for xo in range(width):
                t = pre[xo * rows:(xo + 1) * rows] + column
                cumulative = 0.5 * (1.0 + lax.erf(t * 0.7071067811865476))
                density = jnp.exp(-0.5 * t * t) * 0.3989422804014327
                activated_v[b, :, x + xo, :, zs] = (t * cumulative).astype(BF16).reshape(c, yb, ZC)
                g = cot_v[b, :, x + xo, :, zs].reshape(rows, ZC).astype(F32)
                d_ref[b, centre(x + xo + 1), zs] = (g * (cumulative + t * density)).astype(BF16)

    def backward(b, x, width):
        depth = (width + 2) * 3 * rows
        for m in range(z // ZC):
            zs = slice(m * ZC, (m + 1) * ZC)
            g = jnp.dot(w_back_ref[0:width * rows, 0:depth], d_ref[b, pl.ds(x * 3 * rows, depth), zs],
                        preferred_element_type=F32)
            for xo in range(width):
                part = g[xo * rows:(xo + 1) * rows].astype(BF16)
                grad_v[b, :, x + xo, :, zs] = part.reshape(c, yb, ZC)

    def inner(b):
        for copy in load(b):
            copy.wait()
        for x in range(nx):
            fill(b, x + 1, act_v[b, :, x].reshape(rows, z))
        for x in range(1, nx - 1, 2):
            forward(b, x, 2)
        for x in range(1, nx - 1):
            shift_delta(b, x + 1)

    over_samples(inner)
    acc_ref[...] = jnp.zeros_like(acc_ref)

    def outer(b):
        received_both(face, b)
        fill(b, 0, halo[0, b].reshape(rows, z))
        fill(b, nx + 1, halo[1, b].reshape(rows, z))
        forward(b, 0, 1)
        forward(b, nx - 1, 1)
        @pl.when(b < nb - 1)
        def _():
            start_both(delta, b)

        shift_delta(b, 1)
        shift_delta(b, nx)
        for x in range(nx):
            planes = [s_ref[b, centre(x + i)] for i in range(3)]
            right = jnp.concatenate(planes + [jnp.ones((rows, z), BF16)], axis=0)
            product = lax.dot_general(d_ref[b, pl.ds((x + 1) * 3 * rows, 3 * rows)], right, NT,
                                      preferred_element_type=F32)
            for i in range(4):
                acc_ref[i] += product[:, i * rows:(i + 1) * rows]

    over_samples(outer)

    lane = lax.broadcasted_iota(jnp.int32, (c, rows), 1)
    row = lax.broadcasted_iota(jnp.int32, (c, rows), 0)

    def place(tap, value):
        at, col = tap // 4 * c, tap % 4 * rows
        fold_ref[at:at + c, col:col + rows] = value

    for i in range(3):
        for k in range(3):
            lines = [acc_ref[i, pl.ds(k * rows + y, c, stride=yb), :] for y in range(yb)]
            for j in range(3):
                value = jnp.zeros((c, rows), F32)
                for y in range(yb):
                    if 0 <= y + j - 1 < yb:
                        value = jnp.where(lane % yb == y + j - 1, lines[y], value)
                place((i * 3 + j) * 3 + k, value)
    total = jnp.zeros((c, rows), F32)
    for y in range(yb):
        total = total + acc_ref[3, pl.ds(rows + y, c, stride=yb), :]
    place(27, jnp.where(lane == row * yb, total, 0.0))
    r = lax.broadcasted_iota(jnp.int32, (4 * rows, 4 * c), 0)
    s = lax.broadcasted_iota(jnp.int32, (4 * rows, 4 * c), 1)
    gather = jnp.where(r // yb == s, 1.0, 0.0).astype(F32)
    flat = jnp.dot(fold_ref[...], gather, preferred_element_type=F32, precision=lax.Precision.HIGHEST)
    size = parts.shape[2]
    for at in range(n):
        lo, hi = at * size, min((at + 1) * size, 7 * c)
        filled = max(hi - lo, 0)
        if filled:
            parts[at // chips, at % chips, 0:filled] = flat[lo:hi]
        if filled < size:
            parts[at // chips, at % chips, filled:size] = jnp.zeros((size - filled, 128), F32)
    exchange().start()

    def inner_back(b):
        for x in range(1, nx - 1, 2):
            backward(b, x, 2)

    exchange().wait_recv()
    half[...] = parts[core] + pair[...]
    each_chip(lambda d, to, source: scatter(d, to).start())
    start_both(delta, nb - 1)
    over_samples(inner_back)

    def outer_back(b):
        received_both(delta, b)
        shift_delta(b, 0)
        shift_delta(b, nx + 1)
        backward(b, 0, 1)
        backward(b, nx - 1, 1)

    outer_back(0)
    each_chip(lambda d, to, source: scatter(d, to).wait_recv())
    mine[...] = ((half[chip] + jnp.sum(received[...], axis=0)) * scale).astype(BF16)
    each(lambda d, to, source: spread(d, me, to).start())
    gathered[slot(me)] = mine[...]
    for b in range(1, nb):
        outer_back(b)
    each(lambda d, to, source: spread(d, source, to).wait_recv())
    sums_ref[...] = gathered[...].astype(F32)
    for b in range(nb):
        sent_both(face, b)
        sent_both(delta, b)
    exchange().wait_send()
    each_chip(lambda d, to, source: scatter(d, to).wait_send())
    each(lambda d, to, source: spread(d, me, to).wait_send())


def chunk_rows(c, n):
    rows = 28 * c * c // 128
    return -(-rows // (16 * n)) * 16


def main(activations, cotangent, taps, channel_bias, n, scale):
    nb, c, nx, yb, z = activations.shape
    rows = c * yb
    size = chunk_rows(c, n)
    hbm = pl.BlockSpec(memory_space=pltpu.HBM)
    vmem = pl.BlockSpec(memory_space=pltpu.VMEM)
    dma = pltpu.SemaphoreType.DMA
    block = jax.ShapeDtypeStruct((nb, c, nx, yb, z), BF16)
    return pl.pallas_call(
        functools.partial(main_kernel, n=n, scale=scale),
        in_specs=[hbm, hbm, hbm, hbm],
        out_specs=[vmem, vmem, vmem],
        out_shape=[block, block, jax.ShapeDtypeStruct((n, size, 128), F32)],
        scratch_shapes=[
            pltpu.VMEM((nb, c, nx, yb, z), BF16),
            pltpu.VMEM((nb, c, nx, yb, z), BF16),
            pltpu.VMEM(taps.shape, BF16),
            pltpu.VMEM((1, c), F32),
            pltpu.VMEM((2, nb, c, yb, z), BF16),
            pltpu.VMEM((nb, (nx + 2) * 3 * rows, z), BF16),
            pltpu.VMEM((nb, (nx + 2) * 3 * rows, z), BF16),
            pltpu.VMEM((2 * rows, 12 * rows), BF16),
            pltpu.VMEM((2 * rows, 12 * rows), BF16),
            pltpu.VMEM((4, 3 * rows, rows), F32),
            pltpu.VMEM((7 * c, 4 * rows), F32),
            pltpu.VMEM((2, n // 2, size, 128), F32),
            pltpu.VMEM((n // 2, size, 128), F32),
            pltpu.VMEM((n // 2, size, 128), F32),
            pltpu.VMEM((n // 2 - 1, size, 128), F32),
            pltpu.VMEM((size, 128), BF16),
            pltpu.VMEM((n, size, 128), BF16),
            dma((2, nb)), dma((2,)), dma((2, nb)), dma((2, nb)), dma((2, nb)), dma((2, nb)),
            dma((2,)), dma((n // 2 - 1,)), dma((n // 2 - 1,)), dma((n - 1,)), dma((n - 1,)),
        ],
        compiler_params=pltpu.CompilerParams(
            collective_id=0, has_side_effects=True, vmem_limit_bytes=49 * 1024 * 1024),
        cost_estimate=pl.CostEstimate(flops=10 << 30, bytes_accessed=10 << 20, transcendentals=0),
        name="conv",
    )(activations, cotangent, taps, channel_bias.reshape(1, c))


def finish_kernel(activated_ref, grad_ref, sums_ref, activated_out, grad_out, kernel_out, bias_out,
                  kernel_v, bias_v, sem, small_sem):
    nb = activated_ref.shape[0]
    c = bias_v.shape[1]
    step = c // PIECES
    copies = [pltpu.make_async_copy(src.at[b, p * step:(p + 1) * step], dst.at[b, p * step:(p + 1) * step],
                                    sem.at[w, b, p])
              for b in range(nb) for p in range(PIECES)
              for w, (src, dst) in enumerate(((activated_ref, activated_out), (grad_ref, grad_out)))]
    for copy in copies:
        copy.start()
    flat = sums_ref[...].reshape(-1, 128)
    for tap in range(27):
        row, col = tap // 4 * c, tap % 4 * c
        kernel_v[tap] = flat[row:row + c, col:col + c]
    bias_v[...] = jnp.sum(flat[6 * c:7 * c, 3 * c:4 * c], axis=0, keepdims=True)
    small = (pltpu.make_async_copy(kernel_v, kernel_out, small_sem.at[0]),
             pltpu.make_async_copy(bias_v, bias_out, small_sem.at[1]))
    for copy in small:
        copy.start()
    copies.extend(small)
    for copy in copies:
        copy.wait()


def finish(activated, grad_input, sums):
    nb = activated.shape[0]
    c = activated.shape[1]
    hbm = pl.BlockSpec(memory_space=pl.ANY)
    vmem = pl.BlockSpec(memory_space=pltpu.VMEM)
    block = jax.ShapeDtypeStruct(activated.shape, BF16)
    return pl.pallas_call(
        finish_kernel,
        in_specs=[vmem, vmem, vmem],
        out_specs=[hbm, hbm, hbm, hbm],
        out_shape=[block, block, jax.ShapeDtypeStruct((27, c, c), F32), jax.ShapeDtypeStruct((1, c), F32)],
        scratch_shapes=[pltpu.VMEM((27, c, c), F32), pltpu.VMEM((1, c), F32),
                        pltpu.SemaphoreType.DMA((2, nb, PIECES)), pltpu.SemaphoreType.DMA((2,))],
        compiler_params=pltpu.CompilerParams(vmem_limit_bytes=16 * 1024 * 1024),
        cost_estimate=pl.CostEstimate(flops=1 << 20, bytes_accessed=8 << 20, transcendentals=0),
        name="finish",
    )(activated, grad_input, sums)


def per_device(activations, cotangent, kernel, channel_bias):
    nb, c, nx, yb, z = activations.shape
    n = lax.axis_size("gx")
    taps = jnp.transpose(kernel, (2, 3, 4, 0, 1)).reshape(27, c, c)
    cells = nb * nx * yb * z * n
    taps = pltpu.with_memory_space_constraint(taps, pltpu.HBM)
    channel_bias = pltpu.with_memory_space_constraint(channel_bias.reshape(1, c), pltpu.HBM)
    activated, grad_input, sums = main(activations, cotangent, taps, channel_bias, n, float(cells) ** -0.5)
    activated, grad_input, kernel_sums, bias_sums = finish(activated, grad_input, sums)
    grad_kernel = jnp.transpose(kernel_sums.reshape(3, 3, 3, c, c), (3, 4, 0, 1, 2))
    return activated, grad_input, grad_kernel, bias_sums.reshape(c)


def solution(mesh):
    placed = (P("grp", None, "gx", None, None), P("grp", None, "gx", None, None), P(), P())
    return jax.shard_map(
        per_device,
        mesh=mesh,
        in_specs=placed,
        out_specs=(
            P("grp", None, "gx", None, None),
            P("grp", None, "gx", None, None),
            P("grp", None, None, None, None),
            P("grp"),
        ),
        check_vma=False,
    )
```

```python
import functools

import jax
import jax.numpy as jnp
from jax import lax
from jax.experimental import pallas as pl
from jax.experimental.pallas import tpu as pltpu
from jax.sharding import PartitionSpec as P

F32 = jnp.float32
BF16 = jnp.bfloat16
MESH = pl.DeviceIdType.MESH
NT = (((1,), (1,)), ((), ()))
ZC = 256
PIECES = 4
CUTS = (0, 96, 128)


def one_hot_rows(rows, group, dtype):
    r = lax.broadcasted_iota(jnp.int32, (rows, rows // group), 0)
    c = lax.broadcasted_iota(jnp.int32, (rows, rows // group), 1)
    return jnp.where(r // group == c, 1.0, 0.0).astype(dtype)


def one_hot_cols(rows, group, dtype):
    r = lax.broadcasted_iota(jnp.int32, (rows // group, rows), 0)
    c = lax.broadcasted_iota(jnp.int32, (rows // group, rows), 1)
    return jnp.where(c // group == r, 1.0, 0.0).astype(dtype)


def shifted(v):
    zero = jnp.zeros((v.shape[0], 1), v.dtype)
    return (
        jnp.concatenate([zero, v[:, :-1]], axis=1),
        jnp.concatenate([v[:, 1:], zero], axis=1),
    )


def build_weights(taps_ref, w_ref, w_back_ref, rows, yb):
    c = rows // yb
    spread_rows = one_hot_rows(rows, yb, BF16)
    spread_cols = one_hot_cols(rows, yb, BF16)
    r = lax.broadcasted_iota(jnp.int32, (rows, rows), 0)
    s = lax.broadcasted_iota(jnp.int32, (rows, rows), 1)
    offset = s % yb - r % yb
    wide = jnp.dot(taps_ref[...].reshape(27 * c, c), spread_cols, preferred_element_type=F32).astype(BF16)
    w_ref[...] = jnp.zeros_like(w_ref)
    w_back_ref[...] = jnp.zeros_like(w_back_ref)
    for i in range(3):
        for k in range(3):
            block = jnp.zeros((rows, rows), F32)
            for j in range(3):
                tap = (i * 3 + j) * 3 + k
                full = jnp.dot(spread_rows, wide[tap * c:(tap + 1) * c], preferred_element_type=F32)
                block = jnp.where(offset == j - 1, full, block)
            back = block.T.astype(BF16)
            block = block.astype(BF16)
            for xo in range(2):
                at = slice(xo * rows, (xo + 1) * rows)
                ahead = ((xo + i) * 3 + k) * rows
                behind = ((xo + 2 - i) * 3 + k) * rows
                w_ref[at, ahead:ahead + rows] = block
                w_back_ref[at, behind:behind + rows] = back


def main_kernel(act_ref, cot_ref, taps_ref, bias_ref, activated_v, grad_v, sums_ref,
                act_v, cot_v, taps_v, bias_v, halo, s_ref, d_ref, w_ref, w_back_ref,
                acc_ref, fold_ref, parts, pair, half, received, mine, gathered,
                load_sem, small_sem, face_send, face_recv, delta_send, delta_recv,
                pair_sem, send1, recv1, send2, recv2, *, n, scale):
    nb, c, nx, yb, z = act_v.shape
    rows = c * yb
    me = lax.axis_index("gx")
    up, down = lax.rem(me + 1, n), lax.rem(me + n - 1, n)
    has_down, has_up = me > 0, me < n - 1

    def load(b):
        return (pltpu.make_async_copy(act_ref.at[b], act_v.at[b], load_sem.at[0, b]),
                pltpu.make_async_copy(cot_ref.at[b], cot_v.at[b], load_sem.at[1, b]))

    def face(side, b):
        return pltpu.make_async_remote_copy(
            src_ref=act_ref.at[b, :, nx - 1 if side == 0 else 0], dst_ref=halo.at[side, b],
            send_sem=face_send.at[side, b], recv_sem=face_recv.at[side, b],
            device_id={"gx": up if side == 0 else down}, device_id_type=MESH)

    def centre(slot):
        return pl.ds((slot * 3 + 1) * rows, rows)

    def delta(part):
        def copy(side, b):
            def piece(slot):
                return pl.ds((slot * 3 + 1) * rows + CUTS[part], CUTS[part + 1] - CUTS[part])
            return pltpu.make_async_remote_copy(
                src_ref=d_ref.at[b, piece(nx if side == 0 else 1)],
                dst_ref=d_ref.at[b, piece(0 if side == 0 else nx + 1)],
                send_sem=delta_send.at[side, b, part], recv_sem=delta_recv.at[side, b, part],
                device_id={"gx": up if side == 0 else down}, device_id_type=MESH)
        return copy

    def start_both(copy, b):
        @pl.when(has_up)
        def _():
            copy(0, b).start()

        @pl.when(has_down)
        def _():
            copy(1, b).start()

    def received_both(copy, b):
        @pl.when(has_down)
        def _():
            copy(0, b).wait_recv()

        @pl.when(has_up)
        def _():
            copy(1, b).wait_recv()

    def sent_both(copy, b):
        @pl.when(has_up)
        def _():
            copy(0, b).wait_send()

        @pl.when(has_down)
        def _():
            copy(1, b).wait_send()

    small = (pltpu.make_async_copy(taps_ref, taps_v, small_sem.at[0]),
             pltpu.make_async_copy(bias_ref, bias_v, small_sem.at[1]))

    def each(f):
        def step(d, carry):
            f(d, lax.rem(me + d, n), lax.rem(me + n - d, n))
            return carry
        lax.fori_loop(1, n, step, 0)

    core, chip, chips = lax.rem(me, 2), lax.div(me, 2), n // 2

    def each_chip(f):
        def step(d, carry):
            f(d, lax.rem(chip + d, chips), lax.rem(chip + chips - d, chips))
            return carry
        lax.fori_loop(1, chips, step, 0)

    def exchange():
        return pltpu.make_async_remote_copy(
            src_ref=parts.at[1 - core], dst_ref=pair, send_sem=pair_sem.at[0], recv_sem=pair_sem.at[1],
            device_id={"gx": me + 1 - 2 * core}, device_id_type=MESH)

    def scatter(d, owner):
        return pltpu.make_async_remote_copy(
            src_ref=half.at[owner], dst_ref=received.at[d - 1], send_sem=send1.at[d - 1], recv_sem=recv1.at[d - 1],
            device_id={"gx": 2 * owner + core}, device_id_type=MESH)

    def slot(device):
        return lax.rem(device, 2) * chips + lax.div(device, 2)

    def spread(d, source, peer):
        return pltpu.make_async_remote_copy(
            src_ref=mine, dst_ref=gathered.at[slot(source)], send_sem=send2.at[d - 1], recv_sem=recv2.at[d - 1],
            device_id={"gx": peer}, device_id_type=MESH)

    def over_samples(f):
        def step(b, carry):
            f(b)
            return carry
        lax.fori_loop(0, nb, step, 0)

    for copy in small:
        copy.start()
    for b in range(nb):
        for copy in load(b):
            copy.start()
    barrier = pltpu.get_barrier_semaphore()
    each(lambda d, to, source: pl.semaphore_signal(barrier, inc=1, device_id={"gx": to}, device_id_type=MESH))
    pl.semaphore_wait(barrier, n - 1)
    for b in range(nb):
        start_both(face, b)

    @pl.when(me == 0)
    def _():
        for b in range(nb):
            halo[0, b] = jnp.zeros((c, yb, z), BF16)
            d_ref[b, centre(0)] = jnp.zeros((rows, z), BF16)

    @pl.when(me == n - 1)
    def _():
        for b in range(nb):
            halo[1, b] = jnp.zeros((c, yb, z), BF16)
            d_ref[b, centre(nx + 1)] = jnp.zeros((rows, z), BF16)

    for copy in small:
        copy.wait()
    build_weights(taps_v, w_ref, w_back_ref, rows, yb)
    column = jnp.sum(one_hot_rows(rows, yb, F32) * bias_v[...], axis=1, keepdims=True)

    def fill(b, slot, v):
        before, after = shifted(v)
        for k, part in enumerate((before, v, after)):
            s_ref[b, pl.ds((slot * 3 + k) * rows, rows)] = part

    def shift_delta(b, slot):
        before, after = shifted(d_ref[b, centre(slot)])
        d_ref[b, pl.ds(slot * 3 * rows, rows)] = after
        d_ref[b, pl.ds((slot * 3 + 2) * rows, rows)] = before

    def forward(b, x, width):
        depth = (width + 2) * 3 * rows
        for m in range(z // ZC):
            zs = slice(m * ZC, (m + 1) * ZC)
            pre = jnp.dot(w_ref[0:width * rows, 0:depth], s_ref[b, pl.ds(x * 3 * rows, depth), zs],
                          preferred_element_type=F32)
            for xo in range(width):
                t = pre[xo * rows:(xo + 1) * rows] + column
                cumulative = 0.5 * (1.0 + lax.erf(t * 0.7071067811865476))
                density = jnp.exp(-0.5 * t * t) * 0.3989422804014327
                activated_v[b, :, x + xo, :, zs] = (t * cumulative).astype(BF16).reshape(c, yb, ZC)
                g = cot_v[b, :, x + xo, :, zs].reshape(rows, ZC).astype(F32)
                d_ref[b, centre(x + xo + 1), zs] = (g * (cumulative + t * density)).astype(BF16)

    def backward(b, x, width):
        depth = (width + 2) * 3 * rows
        for m in range(z // ZC):
            zs = slice(m * ZC, (m + 1) * ZC)
            g = jnp.dot(w_back_ref[0:width * rows, 0:depth], d_ref[b, pl.ds(x * 3 * rows, depth), zs],
                        preferred_element_type=F32)
            for xo in range(width):
                part = g[xo * rows:(xo + 1) * rows].astype(BF16)
                grad_v[b, :, x + xo, :, zs] = part.reshape(c, yb, ZC)

    def weight_grad(b, planes_x):
        for x in planes_x:
            planes = [s_ref[b, centre(x + i)] for i in range(3)]
            right = jnp.concatenate(planes + [jnp.ones((rows, z), BF16)], axis=0)
            product = lax.dot_general(d_ref[b, pl.ds((x + 1) * 3 * rows, 3 * rows)], right, NT,
                                      preferred_element_type=F32)
            for i in range(4):
                acc_ref[i] += product[:, i * rows:(i + 1) * rows]

    def inner(b):
        for copy in load(b):
            copy.wait()
        for x in range(nx):
            fill(b, x + 1, act_v[b, :, x].reshape(rows, z))
        for x in range(1, nx - 1, 2):
            forward(b, x, 2)
        for x in range(1, nx - 1):
            shift_delta(b, x + 1)
        weight_grad(b, range(1, nx - 1))

    acc_ref[...] = jnp.zeros_like(acc_ref)
    over_samples(inner)

    def outer(b):
        received_both(face, b)
        fill(b, 0, halo[0, b].reshape(rows, z))
        fill(b, nx + 1, halo[1, b].reshape(rows, z))
        forward(b, 0, 1)
        forward(b, nx - 1, 1)
        @pl.when(b < nb - 1)
        def _():
            start_both(delta(0), b)
            start_both(delta(1), b)

        shift_delta(b, 1)
        shift_delta(b, nx)
        weight_grad(b, (0, nx - 1))

    over_samples(outer)

    lane = lax.broadcasted_iota(jnp.int32, (c, rows), 1)
    row = lax.broadcasted_iota(jnp.int32, (c, rows), 0)

    def place(tap, value):
        at, col = tap // 4 * c, tap % 4 * rows
        fold_ref[at:at + c, col:col + rows] = value

    for i in range(3):
        for k in range(3):
            lines = [acc_ref[i, pl.ds(k * rows + y, c, stride=yb), :] for y in range(yb)]
            for j in range(3):
                value = jnp.zeros((c, rows), F32)
                for y in range(yb):
                    if 0 <= y + j - 1 < yb:
                        value = jnp.where(lane % yb == y + j - 1, lines[y], value)
                place((i * 3 + j) * 3 + k, value)
    total = jnp.zeros((c, rows), F32)
    for y in range(yb):
        total = total + acc_ref[3, pl.ds(rows + y, c, stride=yb), :]
    place(27, jnp.where(lane == row * yb, total, 0.0))
    r = lax.broadcasted_iota(jnp.int32, (4 * rows, 4 * c), 0)
    s = lax.broadcasted_iota(jnp.int32, (4 * rows, 4 * c), 1)
    gather = jnp.where(r // yb == s, 1.0, 0.0).astype(F32)
    flat = jnp.dot(fold_ref[...], gather, preferred_element_type=F32, precision=lax.Precision.HIGHEST)
    size = parts.shape[2]
    for at in range(n):
        lo, hi = at * size, min((at + 1) * size, 7 * c)
        filled = max(hi - lo, 0)
        if filled:
            parts[at // chips, at % chips, 0:filled] = flat[lo:hi]
        if filled < size:
            parts[at // chips, at % chips, filled:size] = jnp.zeros((size - filled, 128), F32)
    exchange().start()

    def inner_back(b):
        for x in range(1, nx - 1, 2):
            backward(b, x, 2)

    exchange().wait_recv()
    half[...] = parts[core] + pair[...]
    each_chip(lambda d, to, source: scatter(d, to).start())
    start_both(delta(0), nb - 1)
    over_samples(inner_back)

    def outer_back(b):
        for part in range(2):
            received_both(delta(part), b)
        shift_delta(b, 0)
        shift_delta(b, nx + 1)
        backward(b, 0, 1)
        backward(b, nx - 1, 1)

    each_chip(lambda d, to, source: scatter(d, to).wait_recv())
    mine[...] = ((half[chip] + jnp.sum(received[...], axis=0)) * scale).astype(BF16)
    each(lambda d, to, source: spread(d, me, to).start())
    start_both(delta(1), nb - 1)
    gathered[slot(me)] = mine[...]
    for b in range(nb):
        outer_back(b)
    each(lambda d, to, source: spread(d, source, to).wait_recv())
    sums_ref[...] = gathered[...].astype(F32)
    for b in range(nb):
        sent_both(face, b)
        for part in range(2):
            sent_both(delta(part), b)
    exchange().wait_send()
    each_chip(lambda d, to, source: scatter(d, to).wait_send())
    each(lambda d, to, source: spread(d, me, to).wait_send())


def chunk_rows(c, n):
    rows = 28 * c * c // 128
    return -(-rows // (16 * n)) * 16


def main(activations, cotangent, taps, channel_bias, n, scale):
    nb, c, nx, yb, z = activations.shape
    rows = c * yb
    size = chunk_rows(c, n)
    hbm = pl.BlockSpec(memory_space=pltpu.HBM)
    vmem = pl.BlockSpec(memory_space=pltpu.VMEM)
    dma = pltpu.SemaphoreType.DMA
    block = jax.ShapeDtypeStruct((nb, c, nx, yb, z), BF16)
    return pl.pallas_call(
        functools.partial(main_kernel, n=n, scale=scale),
        in_specs=[hbm, hbm, hbm, hbm],
        out_specs=[vmem, vmem, vmem],
        out_shape=[block, block, jax.ShapeDtypeStruct((n, size, 128), F32)],
        scratch_shapes=[
            pltpu.VMEM((nb, c, nx, yb, z), BF16),
            pltpu.VMEM((nb, c, nx, yb, z), BF16),
            pltpu.VMEM(taps.shape, BF16),
            pltpu.VMEM((1, c), F32),
            pltpu.VMEM((2, nb, c, yb, z), BF16),
            pltpu.VMEM((nb, (nx + 2) * 3 * rows, z), BF16),
            pltpu.VMEM((nb, (nx + 2) * 3 * rows, z), BF16),
            pltpu.VMEM((2 * rows, 12 * rows), BF16),
            pltpu.VMEM((2 * rows, 12 * rows), BF16),
            pltpu.VMEM((4, 3 * rows, rows), F32),
            pltpu.VMEM((7 * c, 4 * rows), F32),
            pltpu.VMEM((2, n // 2, size, 128), F32),
            pltpu.VMEM((n // 2, size, 128), F32),
            pltpu.VMEM((n // 2, size, 128), F32),
            pltpu.VMEM((n // 2 - 1, size, 128), F32),
            pltpu.VMEM((size, 128), BF16),
            pltpu.VMEM((n, size, 128), BF16),
            dma((2, nb)), dma((2,)), dma((2, nb)), dma((2, nb)), dma((2, nb, 2)), dma((2, nb, 2)),
            dma((2,)), dma((n // 2 - 1,)), dma((n // 2 - 1,)), dma((n - 1,)), dma((n - 1,)),
        ],
        compiler_params=pltpu.CompilerParams(
            collective_id=0, has_side_effects=True, vmem_limit_bytes=49 * 1024 * 1024),
        cost_estimate=pl.CostEstimate(flops=10 << 30, bytes_accessed=10 << 20, transcendentals=0),
        name="conv",
    )(activations, cotangent, taps, channel_bias.reshape(1, c))


def finish_kernel(activated_ref, grad_ref, sums_ref, activated_out, grad_out, kernel_out, bias_out,
                  kernel_v, bias_v, sem, small_sem):
    nb = activated_ref.shape[0]
    c = bias_v.shape[1]
    step = c // PIECES
    copies = [pltpu.make_async_copy(src.at[b, p * step:(p + 1) * step], dst.at[b, p * step:(p + 1) * step],
                                    sem.at[w, b, p])
              for b in range(nb) for p in range(PIECES)
              for w, (src, dst) in enumerate(((activated_ref, activated_out), (grad_ref, grad_out)))]
    for copy in copies:
        copy.start()
    flat = sums_ref[...].reshape(-1, 128)
    for tap in range(27):
        row, col = tap // 4 * c, tap % 4 * c
        kernel_v[tap] = flat[row:row + c, col:col + c]
    bias_v[...] = jnp.sum(flat[6 * c:7 * c, 3 * c:4 * c], axis=0, keepdims=True)
    small = (pltpu.make_async_copy(kernel_v, kernel_out, small_sem.at[0]),
             pltpu.make_async_copy(bias_v, bias_out, small_sem.at[1]))
    for copy in small:
        copy.start()
    copies.extend(small)
    for copy in copies:
        copy.wait()


def finish(activated, grad_input, sums):
    nb = activated.shape[0]
    c = activated.shape[1]
    hbm = pl.BlockSpec(memory_space=pl.ANY)
    vmem = pl.BlockSpec(memory_space=pltpu.VMEM)
    block = jax.ShapeDtypeStruct(activated.shape, BF16)
    return pl.pallas_call(
        finish_kernel,
        in_specs=[vmem, vmem, vmem],
        out_specs=[hbm, hbm, hbm, hbm],
        out_shape=[block, block, jax.ShapeDtypeStruct((27, c, c), F32), jax.ShapeDtypeStruct((1, c), F32)],
        scratch_shapes=[pltpu.VMEM((27, c, c), F32), pltpu.VMEM((1, c), F32),
                        pltpu.SemaphoreType.DMA((2, nb, PIECES)), pltpu.SemaphoreType.DMA((2,))],
        compiler_params=pltpu.CompilerParams(vmem_limit_bytes=16 * 1024 * 1024),
        cost_estimate=pl.CostEstimate(flops=1 << 20, bytes_accessed=8 << 20, transcendentals=0),
        name="finish",
    )(activated, grad_input, sums)


def per_device(activations, cotangent, kernel, channel_bias):
    nb, c, nx, yb, z = activations.shape
    n = lax.axis_size("gx")
    taps = jnp.transpose(kernel, (2, 3, 4, 0, 1)).reshape(27, c, c)
    cells = nb * nx * yb * z * n
    taps = pltpu.with_memory_space_constraint(taps, pltpu.HBM)
    channel_bias = pltpu.with_memory_space_constraint(channel_bias.reshape(1, c), pltpu.HBM)
    activated, grad_input, sums = main(activations, cotangent, taps, channel_bias, n, float(cells) ** -0.5)
    activated, grad_input, kernel_sums, bias_sums = finish(activated, grad_input, sums)
    grad_kernel = jnp.transpose(kernel_sums.reshape(3, 3, 3, c, c), (3, 4, 0, 1, 2))
    return activated, grad_input, grad_kernel, bias_sums.reshape(c)


def solution(mesh):
    placed = (P("grp", None, "gx", None, None), P("grp", None, "gx", None, None), P(), P())
    return jax.shard_map(
        per_device,
        mesh=mesh,
        in_specs=placed,
        out_specs=(
            P("grp", None, "gx", None, None),
            P("grp", None, "gx", None, None),
            P("grp", None, None, None, None),
            P("grp"),
        ),
        check_vma=False,
    )
```

```python
import functools

import jax
import jax.numpy as jnp
from jax import lax
from jax.experimental import pallas as pl
from jax.experimental.pallas import tpu as pltpu
from jax.sharding import PartitionSpec as P

F32 = jnp.float32
BF16 = jnp.bfloat16
MESH = pl.DeviceIdType.MESH
NT = (((1,), (1,)), ((), ()))
ZC = 256
PIECES = 4
CUTS = (0, 96, 128)


def one_hot_rows(rows, group, dtype):
    r = lax.broadcasted_iota(jnp.int32, (rows, rows // group), 0)
    c = lax.broadcasted_iota(jnp.int32, (rows, rows // group), 1)
    return jnp.where(r // group == c, 1.0, 0.0).astype(dtype)


def one_hot_cols(rows, group, dtype):
    r = lax.broadcasted_iota(jnp.int32, (rows // group, rows), 0)
    c = lax.broadcasted_iota(jnp.int32, (rows // group, rows), 1)
    return jnp.where(c // group == r, 1.0, 0.0).astype(dtype)


def shifted(v):
    zero = jnp.zeros((v.shape[0], 1), v.dtype)
    return (
        jnp.concatenate([zero, v[:, :-1]], axis=1),
        jnp.concatenate([v[:, 1:], zero], axis=1),
    )


def build_weights(taps_ref, w_ref, w_back_ref, rows, yb):
    c = rows // yb
    spread_rows = one_hot_rows(rows, yb, BF16)
    spread_cols = one_hot_cols(rows, yb, BF16)
    r = lax.broadcasted_iota(jnp.int32, (rows, rows), 0)
    s = lax.broadcasted_iota(jnp.int32, (rows, rows), 1)
    offset = s % yb - r % yb
    wide = jnp.dot(taps_ref[...].reshape(27 * c, c), spread_cols, preferred_element_type=F32).astype(BF16)
    w_ref[...] = jnp.zeros_like(w_ref)
    w_back_ref[...] = jnp.zeros_like(w_back_ref)
    for i in range(3):
        for k in range(3):
            block = jnp.zeros((rows, rows), F32)
            for j in range(3):
                tap = (i * 3 + j) * 3 + k
                full = jnp.dot(spread_rows, wide[tap * c:(tap + 1) * c], preferred_element_type=F32)
                block = jnp.where(offset == j - 1, full, block)
            back = block.T.astype(BF16)
            block = block.astype(BF16)
            for xo in range(2):
                at = slice(xo * rows, (xo + 1) * rows)
                ahead = ((xo + i) * 3 + k) * rows
                behind = ((xo + 2 - i) * 3 + k) * rows
                w_ref[at, ahead:ahead + rows] = block
                w_back_ref[at, behind:behind + rows] = back


def main_kernel(act_ref, cot_ref, taps_ref, bias_ref, activated_v, grad_v, sums_ref,
                act_v, cot_v, taps_v, bias_v, halo, s_ref, d_ref, begun_ref, w_ref, w_back_ref,
                acc_ref, fold_ref, parts, pair, half, received, mine, gathered,
                load_sem, small_sem, face_send, face_recv, delta_send, delta_recv,
                pair_sem, send1, recv1, send2, recv2, *, n, scale):
    nb, c, nx, yb, z = act_v.shape
    rows = c * yb
    me = lax.axis_index("gx")
    up, down = lax.rem(me + 1, n), lax.rem(me + n - 1, n)
    has_down, has_up = me > 0, me < n - 1

    def load(b):
        return (pltpu.make_async_copy(act_ref.at[b], act_v.at[b], load_sem.at[0, b]),
                pltpu.make_async_copy(cot_ref.at[b], cot_v.at[b], load_sem.at[1, b]))

    def face(side, b):
        return pltpu.make_async_remote_copy(
            src_ref=act_ref.at[b, :, nx - 1 if side == 0 else 0], dst_ref=halo.at[side, b],
            send_sem=face_send.at[side, b], recv_sem=face_recv.at[side, b],
            device_id={"gx": up if side == 0 else down}, device_id_type=MESH)

    def centre(slot):
        return pl.ds((slot * 3 + 1) * rows, rows)

    def delta(part):
        def copy(side, b):
            def piece(slot):
                return pl.ds((slot * 3 + 1) * rows + CUTS[part], CUTS[part + 1] - CUTS[part])
            return pltpu.make_async_remote_copy(
                src_ref=d_ref.at[b, piece(nx if side == 0 else 1)],
                dst_ref=d_ref.at[b, piece(0 if side == 0 else nx + 1)],
                send_sem=delta_send.at[side, b, part], recv_sem=delta_recv.at[side, b, part],
                device_id={"gx": up if side == 0 else down}, device_id_type=MESH)
        return copy

    def start_both(copy, b):
        @pl.when(has_up)
        def _():
            copy(0, b).start()

        @pl.when(has_down)
        def _():
            copy(1, b).start()

    def received_both(copy, b):
        @pl.when(has_down)
        def _():
            copy(0, b).wait_recv()

        @pl.when(has_up)
        def _():
            copy(1, b).wait_recv()

    def sent_both(copy, b):
        @pl.when(has_up)
        def _():
            copy(0, b).wait_send()

        @pl.when(has_down)
        def _():
            copy(1, b).wait_send()

    small = (pltpu.make_async_copy(taps_ref, taps_v, small_sem.at[0]),
             pltpu.make_async_copy(bias_ref, bias_v, small_sem.at[1]))

    def each(f):
        def step(d, carry):
            f(d, lax.rem(me + d, n), lax.rem(me + n - d, n))
            return carry
        lax.fori_loop(1, n, step, 0)

    core, chip, chips = lax.rem(me, 2), lax.div(me, 2), n // 2

    def each_chip(f):
        def step(d, carry):
            f(d, lax.rem(chip + d, chips), lax.rem(chip + chips - d, chips))
            return carry
        lax.fori_loop(1, chips, step, 0)

    def exchange():
        return pltpu.make_async_remote_copy(
            src_ref=parts.at[1 - core], dst_ref=pair, send_sem=pair_sem.at[0], recv_sem=pair_sem.at[1],
            device_id={"gx": me + 1 - 2 * core}, device_id_type=MESH)

    def scatter(d, owner):
        return pltpu.make_async_remote_copy(
            src_ref=half.at[owner], dst_ref=received.at[d - 1], send_sem=send1.at[d - 1], recv_sem=recv1.at[d - 1],
            device_id={"gx": 2 * owner + core}, device_id_type=MESH)

    def slot(device):
        return lax.rem(device, 2) * chips + lax.div(device, 2)

    def spread(d, source, peer):
        return pltpu.make_async_remote_copy(
            src_ref=mine, dst_ref=gathered.at[slot(source)], send_sem=send2.at[d - 1], recv_sem=recv2.at[d - 1],
            device_id={"gx": peer}, device_id_type=MESH)

    def over_samples(f):
        def step(b, carry):
            f(b)
            return carry
        lax.fori_loop(0, nb, step, 0)

    for copy in small:
        copy.start()
    for b in range(nb):
        for copy in load(b):
            copy.start()
    barrier = pltpu.get_barrier_semaphore()
    each(lambda d, to, source: pl.semaphore_signal(barrier, inc=1, device_id={"gx": to}, device_id_type=MESH))
    pl.semaphore_wait(barrier, n - 1)
    for b in range(nb):
        start_both(face, b)

    @pl.when(me == 0)
    def _():
        for b in range(nb):
            halo[0, b] = jnp.zeros((c, yb, z), BF16)
            d_ref[b, centre(0)] = jnp.zeros((rows, z), BF16)

    @pl.when(me == n - 1)
    def _():
        for b in range(nb):
            halo[1, b] = jnp.zeros((c, yb, z), BF16)
            d_ref[b, centre(nx + 1)] = jnp.zeros((rows, z), BF16)

    for copy in small:
        copy.wait()
    build_weights(taps_v, w_ref, w_back_ref, rows, yb)
    column = jnp.sum(one_hot_rows(rows, yb, F32) * bias_v[...], axis=1, keepdims=True)

    def fill(b, slot, v):
        before, after = shifted(v)
        for k, part in enumerate((before, v, after)):
            s_ref[b, pl.ds((slot * 3 + k) * rows, rows)] = part

    def shift_delta(b, slot):
        before, after = shifted(d_ref[b, centre(slot)])
        d_ref[b, pl.ds(slot * 3 * rows, rows)] = after
        d_ref[b, pl.ds((slot * 3 + 2) * rows, rows)] = before

    def product(b, start, first, depth, height, zs):
        return jnp.dot(w_ref[0:height, first:first + depth], s_ref[b, pl.ds(start, depth), zs],
                       preferred_element_type=F32)

    def finish_plane(b, x, pre, zs):
        t = pre + column
        cumulative = 0.5 * (1.0 + lax.erf(t * 0.7071067811865476))
        density = jnp.exp(-0.5 * t * t) * 0.3989422804014327
        activated_v[b, :, x, :, zs] = (t * cumulative).astype(BF16).reshape(c, yb, ZC)
        g = cot_v[b, :, x, :, zs].reshape(rows, ZC).astype(F32)
        d_ref[b, centre(x + 1), zs] = (g * (cumulative + t * density)).astype(BF16)

    def forward(b, x):
        for m in range(z // ZC):
            zs = slice(m * ZC, (m + 1) * ZC)
            pre = product(b, x * 3 * rows, 0, 12 * rows, 2 * rows, zs)
            for xo in range(2):
                finish_plane(b, x + xo, pre[xo * rows:(xo + 1) * rows], zs)

    def begin_faces(b):
        for m in range(z // ZC):
            zs = slice(m * ZC, (m + 1) * ZC)
            begun_ref[b, 0, :, zs] = product(b, 3 * rows, 3 * rows, 6 * rows, rows, zs)
            begun_ref[b, 1, :, zs] = product(b, (nx - 1) * 3 * rows, 0, 6 * rows, rows, zs)

    def end_faces(b):
        for m in range(z // ZC):
            zs = slice(m * ZC, (m + 1) * ZC)
            finish_plane(b, 0, begun_ref[b, 0, :, zs] + product(b, 0, 0, 3 * rows, rows, zs), zs)
            finish_plane(b, nx - 1, begun_ref[b, 1, :, zs]
                         + product(b, (nx + 1) * 3 * rows, 6 * rows, 3 * rows, rows, zs), zs)

    def backward(b, x, width):
        depth = (width + 2) * 3 * rows
        for m in range(z // ZC):
            zs = slice(m * ZC, (m + 1) * ZC)
            g = jnp.dot(w_back_ref[0:width * rows, 0:depth], d_ref[b, pl.ds(x * 3 * rows, depth), zs],
                        preferred_element_type=F32)
            for xo in range(width):
                part = g[xo * rows:(xo + 1) * rows].astype(BF16)
                grad_v[b, :, x + xo, :, zs] = part.reshape(c, yb, ZC)

    def weight_grad(b, planes_x):
        for x in planes_x:
            planes = [s_ref[b, centre(x + i)] for i in range(3)]
            right = jnp.concatenate(planes + [jnp.ones((rows, z), BF16)], axis=0)
            product = lax.dot_general(d_ref[b, pl.ds((x + 1) * 3 * rows, 3 * rows)], right, NT,
                                      preferred_element_type=F32)
            for i in range(4):
                acc_ref[i] += product[:, i * rows:(i + 1) * rows]

    def inner(b):
        for copy in load(b):
            copy.wait()
        for x in range(nx):
            fill(b, x + 1, act_v[b, :, x].reshape(rows, z))
        for x in range(1, nx - 1, 2):
            forward(b, x)
        for x in range(1, nx - 1):
            shift_delta(b, x + 1)
        weight_grad(b, range(1, nx - 1))
        begin_faces(b)

    acc_ref[...] = jnp.zeros_like(acc_ref)
    over_samples(inner)

    def outer(b):
        received_both(face, b)
        fill(b, 0, halo[0, b].reshape(rows, z))
        fill(b, nx + 1, halo[1, b].reshape(rows, z))
        end_faces(b)
        @pl.when(b < nb - 1)
        def _():
            start_both(delta(0), b)
            start_both(delta(1), b)

        shift_delta(b, 1)
        shift_delta(b, nx)
        weight_grad(b, (0, nx - 1))

    over_samples(outer)

    lane = lax.broadcasted_iota(jnp.int32, (c, rows), 1)
    row = lax.broadcasted_iota(jnp.int32, (c, rows), 0)

    def place(tap, value):
        at, col = tap // 4 * c, tap % 4 * rows
        fold_ref[at:at + c, col:col + rows] = value

    for i in range(3):
        for k in range(3):
            lines = [acc_ref[i, pl.ds(k * rows + y, c, stride=yb), :] for y in range(yb)]
            for j in range(3):
                value = jnp.zeros((c, rows), F32)
                for y in range(yb):
                    if 0 <= y + j - 1 < yb:
                        value = jnp.where(lane % yb == y + j - 1, lines[y], value)
                place((i * 3 + j) * 3 + k, value)
    total = jnp.zeros((c, rows), F32)
    for y in range(yb):
        total = total + acc_ref[3, pl.ds(rows + y, c, stride=yb), :]
    place(27, jnp.where(lane == row * yb, total, 0.0))
    r = lax.broadcasted_iota(jnp.int32, (4 * rows, 4 * c), 0)
    s = lax.broadcasted_iota(jnp.int32, (4 * rows, 4 * c), 1)
    gather = jnp.where(r // yb == s, 1.0, 0.0).astype(F32)
    flat = jnp.dot(fold_ref[...], gather, preferred_element_type=F32, precision=lax.Precision.HIGHEST)
    size = parts.shape[2]
    for at in range(n):
        lo, hi = at * size, min((at + 1) * size, 7 * c)
        filled = max(hi - lo, 0)
        if filled:
            parts[at // chips, at % chips, 0:filled] = flat[lo:hi]
        if filled < size:
            parts[at // chips, at % chips, filled:size] = jnp.zeros((size - filled, 128), F32)
    exchange().start()

    def inner_back(b):
        for x in range(1, nx - 1, 2):
            backward(b, x, 2)

    exchange().wait_recv()
    half[...] = parts[core] + pair[...]
    each_chip(lambda d, to, source: scatter(d, to).start())
    start_both(delta(0), nb - 1)
    over_samples(inner_back)

    def outer_back(b):
        for part in range(2):
            received_both(delta(part), b)
        shift_delta(b, 0)
        shift_delta(b, nx + 1)
        backward(b, 0, 1)
        backward(b, nx - 1, 1)

    each_chip(lambda d, to, source: scatter(d, to).wait_recv())
    mine[...] = ((half[chip] + jnp.sum(received[...], axis=0)) * scale).astype(BF16)
    each(lambda d, to, source: spread(d, me, to).start())
    start_both(delta(1), nb - 1)
    gathered[slot(me)] = mine[...]
    for b in range(nb):
        outer_back(b)
    each(lambda d, to, source: spread(d, source, to).wait_recv())
    sums_ref[...] = gathered[...].astype(F32)
    for b in range(nb):
        sent_both(face, b)
        for part in range(2):
            sent_both(delta(part), b)
    exchange().wait_send()
    each_chip(lambda d, to, source: scatter(d, to).wait_send())
    each(lambda d, to, source: spread(d, me, to).wait_send())


def chunk_rows(c, n):
    rows = 28 * c * c // 128
    return -(-rows // (16 * n)) * 16


def main(activations, cotangent, taps, channel_bias, n, scale):
    nb, c, nx, yb, z = activations.shape
    rows = c * yb
    size = chunk_rows(c, n)
    hbm = pl.BlockSpec(memory_space=pltpu.HBM)
    vmem = pl.BlockSpec(memory_space=pltpu.VMEM)
    dma = pltpu.SemaphoreType.DMA
    block = jax.ShapeDtypeStruct((nb, c, nx, yb, z), BF16)
    return pl.pallas_call(
        functools.partial(main_kernel, n=n, scale=scale),
        in_specs=[hbm, hbm, hbm, hbm],
        out_specs=[vmem, vmem, vmem],
        out_shape=[block, block, jax.ShapeDtypeStruct((n, size, 128), F32)],
        scratch_shapes=[
            pltpu.VMEM((nb, c, nx, yb, z), BF16),
            pltpu.VMEM((nb, c, nx, yb, z), BF16),
            pltpu.VMEM(taps.shape, BF16),
            pltpu.VMEM((1, c), F32),
            pltpu.VMEM((2, nb, c, yb, z), BF16),
            pltpu.VMEM((nb, (nx + 2) * 3 * rows, z), BF16),
            pltpu.VMEM((nb, (nx + 2) * 3 * rows, z), BF16),
            pltpu.VMEM((nb, 2, rows, z), F32),
            pltpu.VMEM((2 * rows, 12 * rows), BF16),
            pltpu.VMEM((2 * rows, 12 * rows), BF16),
            pltpu.VMEM((4, 3 * rows, rows), F32),
            pltpu.VMEM((7 * c, 4 * rows), F32),
            pltpu.VMEM((2, n // 2, size, 128), F32),
            pltpu.VMEM((n // 2, size, 128), F32),
            pltpu.VMEM((n // 2, size, 128), F32),
            pltpu.VMEM((n // 2 - 1, size, 128), F32),
            pltpu.VMEM((size, 128), BF16),
            pltpu.VMEM((n, size, 128), BF16),
            dma((2, nb)), dma((2,)), dma((2, nb)), dma((2, nb)), dma((2, nb, 2)), dma((2, nb, 2)),
            dma((2,)), dma((n // 2 - 1,)), dma((n // 2 - 1,)), dma((n - 1,)), dma((n - 1,)),
        ],
        compiler_params=pltpu.CompilerParams(
            collective_id=0, has_side_effects=True, vmem_limit_bytes=49 * 1024 * 1024),
        cost_estimate=pl.CostEstimate(flops=10 << 30, bytes_accessed=10 << 20, transcendentals=0),
        name="conv",
    )(activations, cotangent, taps, channel_bias.reshape(1, c))


def finish_kernel(activated_ref, grad_ref, sums_ref, activated_out, grad_out, kernel_out, bias_out,
                  kernel_v, bias_v, sem, small_sem):
    nb = activated_ref.shape[0]
    c = bias_v.shape[1]
    step = c // PIECES
    copies = [pltpu.make_async_copy(src.at[b, p * step:(p + 1) * step], dst.at[b, p * step:(p + 1) * step],
                                    sem.at[w, b, p])
              for b in range(nb) for p in range(PIECES)
              for w, (src, dst) in enumerate(((activated_ref, activated_out), (grad_ref, grad_out)))]
    for copy in copies:
        copy.start()
    flat = sums_ref[...].reshape(-1, 128)
    for tap in range(27):
        row, col = tap // 4 * c, tap % 4 * c
        kernel_v[tap] = flat[row:row + c, col:col + c]
    bias_v[...] = jnp.sum(flat[6 * c:7 * c, 3 * c:4 * c], axis=0, keepdims=True)
    small = (pltpu.make_async_copy(kernel_v, kernel_out, small_sem.at[0]),
             pltpu.make_async_copy(bias_v, bias_out, small_sem.at[1]))
    for copy in small:
        copy.start()
    copies.extend(small)
    for copy in copies:
        copy.wait()


def finish(activated, grad_input, sums):
    nb = activated.shape[0]
    c = activated.shape[1]
    hbm = pl.BlockSpec(memory_space=pl.ANY)
    vmem = pl.BlockSpec(memory_space=pltpu.VMEM)
    block = jax.ShapeDtypeStruct(activated.shape, BF16)
    return pl.pallas_call(
        finish_kernel,
        in_specs=[vmem, vmem, vmem],
        out_specs=[hbm, hbm, hbm, hbm],
        out_shape=[block, block, jax.ShapeDtypeStruct((27, c, c), F32), jax.ShapeDtypeStruct((1, c), F32)],
        scratch_shapes=[pltpu.VMEM((27, c, c), F32), pltpu.VMEM((1, c), F32),
                        pltpu.SemaphoreType.DMA((2, nb, PIECES)), pltpu.SemaphoreType.DMA((2,))],
        compiler_params=pltpu.CompilerParams(vmem_limit_bytes=16 * 1024 * 1024),
        cost_estimate=pl.CostEstimate(flops=1 << 20, bytes_accessed=8 << 20, transcendentals=0),
        name="finish",
    )(activated, grad_input, sums)


def per_device(activations, cotangent, kernel, channel_bias):
    nb, c, nx, yb, z = activations.shape
    n = lax.axis_size("gx")
    taps = jnp.transpose(kernel, (2, 3, 4, 0, 1)).reshape(27, c, c)
    cells = nb * nx * yb * z * n
    taps = pltpu.with_memory_space_constraint(taps, pltpu.HBM)
    channel_bias = pltpu.with_memory_space_constraint(channel_bias.reshape(1, c), pltpu.HBM)
    activated, grad_input, sums = main(activations, cotangent, taps, channel_bias, n, float(cells) ** -0.5)
    activated, grad_input, kernel_sums, bias_sums = finish(activated, grad_input, sums)
    grad_kernel = jnp.transpose(kernel_sums.reshape(3, 3, 3, c, c), (3, 4, 0, 1, 2))
    return activated, grad_input, grad_kernel, bias_sums.reshape(c)


def solution(mesh):
    placed = (P("grp", None, "gx", None, None), P("grp", None, "gx", None, None), P(), P())
    return jax.shard_map(
        per_device,
        mesh=mesh,
        in_specs=placed,
        out_specs=(
            P("grp", None, "gx", None, None),
            P("grp", None, "gx", None, None),
            P("grp", None, None, None, None),
            P("grp"),
        ),
        check_vma=False,
    )
```

```python
import functools

import jax
import jax.numpy as jnp
from jax import lax
from jax.experimental import pallas as pl
from jax.experimental.pallas import tpu as pltpu
from jax.sharding import PartitionSpec as P

F32 = jnp.float32
BF16 = jnp.bfloat16
MESH = pl.DeviceIdType.MESH
NT = (((1,), (1,)), ((), ()))
ZC = 256
PIECES = 4
CUTS = (0, 96, 128)


def one_hot_rows(rows, group, dtype):
    r = lax.broadcasted_iota(jnp.int32, (rows, rows // group), 0)
    c = lax.broadcasted_iota(jnp.int32, (rows, rows // group), 1)
    return jnp.where(r // group == c, 1.0, 0.0).astype(dtype)


def one_hot_cols(rows, group, dtype):
    r = lax.broadcasted_iota(jnp.int32, (rows // group, rows), 0)
    c = lax.broadcasted_iota(jnp.int32, (rows // group, rows), 1)
    return jnp.where(c // group == r, 1.0, 0.0).astype(dtype)


def shifted(v):
    zero = jnp.zeros((v.shape[0], 1), v.dtype)
    return (
        jnp.concatenate([zero, v[:, :-1]], axis=1),
        jnp.concatenate([v[:, 1:], zero], axis=1),
    )


def build_weights(taps_ref, w_ref, w_back_ref, rows, yb):
    c = rows // yb
    spread_rows = one_hot_rows(rows, yb, BF16)
    spread_cols = one_hot_cols(rows, yb, BF16)
    r = lax.broadcasted_iota(jnp.int32, (rows, rows), 0)
    s = lax.broadcasted_iota(jnp.int32, (rows, rows), 1)
    offset = s % yb - r % yb
    wide = jnp.dot(taps_ref[...].reshape(27 * c, c), spread_cols, preferred_element_type=F32).astype(BF16)
    w_ref[...] = jnp.zeros_like(w_ref)
    w_back_ref[...] = jnp.zeros_like(w_back_ref)
    for i in range(3):
        for k in range(3):
            block = jnp.zeros((rows, rows), F32)
            for j in range(3):
                tap = (i * 3 + j) * 3 + k
                full = jnp.dot(spread_rows, wide[tap * c:(tap + 1) * c], preferred_element_type=F32)
                block = jnp.where(offset == j - 1, full, block)
            back = block.T.astype(BF16)
            block = block.astype(BF16)
            for xo in range(2):
                at = slice(xo * rows, (xo + 1) * rows)
                ahead = ((xo + i) * 3 + k) * rows
                behind = ((xo + 2 - i) * 3 + k) * rows
                w_ref[at, ahead:ahead + rows] = block
                w_back_ref[at, behind:behind + rows] = back


def main_kernel(act_ref, cot_ref, taps_ref, bias_ref, activated_v, grad_v, sums_ref,
                act_v, cot_v, taps_v, bias_v, halo, s_ref, d_ref, begun_ref, w_ref, w_back_ref,
                acc_ref, fold_ref, parts, pair, half, received, mine, gathered,
                load_sem, small_sem, face_send, face_recv, delta_send, delta_recv,
                pair_sem, send1, recv1, send2, recv2, *, n, scale):
    nb, c, nx, yb, z = act_v.shape
    rows = c * yb
    me = lax.axis_index("gx")
    up, down = lax.rem(me + 1, n), lax.rem(me + n - 1, n)
    has_down, has_up = me > 0, me < n - 1

    def load(b):
        return (pltpu.make_async_copy(act_ref.at[b], act_v.at[b], load_sem.at[0, b]),
                pltpu.make_async_copy(cot_ref.at[b], cot_v.at[b], load_sem.at[1, b]))

    def face(side, b):
        return pltpu.make_async_remote_copy(
            src_ref=act_ref.at[b, :, nx - 1 if side == 0 else 0], dst_ref=halo.at[side, b],
            send_sem=face_send.at[side, b], recv_sem=face_recv.at[side, b],
            device_id={"gx": up if side == 0 else down}, device_id_type=MESH)

    def centre(slot):
        return pl.ds((slot * 3 + 1) * rows, rows)

    def delta(part):
        def copy(side, b):
            def piece(slot):
                return pl.ds((slot * 3 + 1) * rows + CUTS[part], CUTS[part + 1] - CUTS[part])
            return pltpu.make_async_remote_copy(
                src_ref=d_ref.at[b, piece(nx if side == 0 else 1)],
                dst_ref=d_ref.at[b, piece(0 if side == 0 else nx + 1)],
                send_sem=delta_send.at[side, b, part], recv_sem=delta_recv.at[side, b, part],
                device_id={"gx": up if side == 0 else down}, device_id_type=MESH)
        return copy

    def start_both(copy, b):
        @pl.when(has_up)
        def _():
            copy(0, b).start()

        @pl.when(has_down)
        def _():
            copy(1, b).start()

    def received_both(copy, b):
        @pl.when(has_down)
        def _():
            copy(0, b).wait_recv()

        @pl.when(has_up)
        def _():
            copy(1, b).wait_recv()

    def sent_both(copy, b):
        @pl.when(has_up)
        def _():
            copy(0, b).wait_send()

        @pl.when(has_down)
        def _():
            copy(1, b).wait_send()

    small = (pltpu.make_async_copy(taps_ref, taps_v, small_sem.at[0]),
             pltpu.make_async_copy(bias_ref, bias_v, small_sem.at[1]))

    def each(f):
        def step(d, carry):
            f(d, lax.rem(me + d, n), lax.rem(me + n - d, n))
            return carry
        lax.fori_loop(1, n, step, 0)

    core, chip, chips = lax.rem(me, 2), lax.div(me, 2), n // 2

    def each_chip(f):
        def step(d, carry):
            f(d, lax.rem(chip + d, chips), lax.rem(chip + chips - d, chips))
            return carry
        lax.fori_loop(1, chips, step, 0)

    def exchange():
        return pltpu.make_async_remote_copy(
            src_ref=parts.at[1 - core], dst_ref=pair, send_sem=pair_sem.at[0], recv_sem=pair_sem.at[1],
            device_id={"gx": me + 1 - 2 * core}, device_id_type=MESH)

    def scatter(d, owner):
        return pltpu.make_async_remote_copy(
            src_ref=half.at[owner], dst_ref=received.at[d - 1], send_sem=send1.at[d - 1], recv_sem=recv1.at[d - 1],
            device_id={"gx": 2 * owner + core}, device_id_type=MESH)

    def slot(device):
        return lax.rem(device, 2) * chips + lax.div(device, 2)

    def spread(d, source, peer):
        return pltpu.make_async_remote_copy(
            src_ref=mine, dst_ref=gathered.at[slot(source)], send_sem=send2.at[d - 1], recv_sem=recv2.at[d - 1],
            device_id={"gx": peer}, device_id_type=MESH)

    def over_samples(f):
        def step(b, carry):
            f(b)
            return carry
        lax.fori_loop(0, nb, step, 0)

    for copy in small:
        copy.start()
    for b in range(nb):
        for copy in load(b):
            copy.start()
    barrier = pltpu.get_barrier_semaphore()
    each(lambda d, to, source: pl.semaphore_signal(barrier, inc=1, device_id={"gx": to}, device_id_type=MESH))
    pl.semaphore_wait(barrier, n - 1)
    for b in range(nb):
        start_both(face, b)

    @pl.when(me == 0)
    def _():
        for b in range(nb):
            halo[0, b] = jnp.zeros((c, yb, z), BF16)
            d_ref[b, centre(0)] = jnp.zeros((rows, z), BF16)

    @pl.when(me == n - 1)
    def _():
        for b in range(nb):
            halo[1, b] = jnp.zeros((c, yb, z), BF16)
            d_ref[b, centre(nx + 1)] = jnp.zeros((rows, z), BF16)

    for copy in small:
        copy.wait()
    build_weights(taps_v, w_ref, w_back_ref, rows, yb)
    column = jnp.sum(one_hot_rows(rows, yb, F32) * bias_v[...], axis=1, keepdims=True)

    def fill(b, slot, v):
        before, after = shifted(v)
        for k, part in enumerate((before, v, after)):
            s_ref[b, pl.ds((slot * 3 + k) * rows, rows)] = part

    def shift_delta(b, slot):
        before, after = shifted(d_ref[b, centre(slot)])
        d_ref[b, pl.ds(slot * 3 * rows, rows)] = after
        d_ref[b, pl.ds((slot * 3 + 2) * rows, rows)] = before

    def product(b, start, first, depth, height, zs):
        return jnp.dot(w_ref[0:height, first:first + depth], s_ref[b, pl.ds(start, depth), zs],
                       preferred_element_type=F32)

    def finish_plane(b, x, pre, zs):
        t = pre + column
        cumulative = 0.5 * (1.0 + lax.erf(t * 0.7071067811865476))
        density = jnp.exp(-0.5 * t * t) * 0.3989422804014327
        activated_v[b, :, x, :, zs] = (t * cumulative).astype(BF16).reshape(c, yb, ZC)
        g = cot_v[b, :, x, :, zs].reshape(rows, ZC).astype(F32)
        d_ref[b, centre(x + 1), zs] = (g * (cumulative + t * density)).astype(BF16)

    def forward(b, x):
        for m in range(z // ZC):
            zs = slice(m * ZC, (m + 1) * ZC)
            pre = product(b, x * 3 * rows, 0, 12 * rows, 2 * rows, zs)
            for xo in range(2):
                finish_plane(b, x + xo, pre[xo * rows:(xo + 1) * rows], zs)

    def begin_faces(b):
        for m in range(z // ZC):
            zs = slice(m * ZC, (m + 1) * ZC)
            begun_ref[b, 0, :, zs] = product(b, 3 * rows, 3 * rows, 6 * rows, rows, zs)
            begun_ref[b, 1, :, zs] = product(b, (nx - 1) * 3 * rows, 0, 6 * rows, rows, zs)

    def end_faces(b):
        for m in range(z // ZC):
            zs = slice(m * ZC, (m + 1) * ZC)
            finish_plane(b, 0, begun_ref[b, 0, :, zs] + product(b, 0, 0, 3 * rows, rows, zs), zs)
            finish_plane(b, nx - 1, begun_ref[b, 1, :, zs]
                         + product(b, (nx + 1) * 3 * rows, 6 * rows, 3 * rows, rows, zs), zs)

    def product_back(b, start, first, depth, height, zs):
        return jnp.dot(w_back_ref[0:height, first:first + depth], d_ref[b, pl.ds(start, depth), zs],
                       preferred_element_type=F32)

    def backward(b, x):
        for m in range(z // ZC):
            zs = slice(m * ZC, (m + 1) * ZC)
            g = product_back(b, x * 3 * rows, 0, 12 * rows, 2 * rows, zs)
            for xo in range(2):
                grad_v[b, :, x + xo, :, zs] = g[xo * rows:(xo + 1) * rows].astype(BF16).reshape(c, yb, ZC)

    def begin_back_faces(b):
        for m in range(z // ZC):
            zs = slice(m * ZC, (m + 1) * ZC)
            begun_ref[b, 0, :, zs] = product_back(b, 3 * rows, 3 * rows, 6 * rows, rows, zs)
            begun_ref[b, 1, :, zs] = product_back(b, (nx - 1) * 3 * rows, 0, 6 * rows, rows, zs)

    def end_back_faces(b):
        for m in range(z // ZC):
            zs = slice(m * ZC, (m + 1) * ZC)
            g = begun_ref[b, 0, :, zs] + product_back(b, 0, 0, 3 * rows, rows, zs)
            grad_v[b, :, 0, :, zs] = g.astype(BF16).reshape(c, yb, ZC)
            g = begun_ref[b, 1, :, zs] + product_back(b, (nx + 1) * 3 * rows, 6 * rows, 3 * rows, rows, zs)
            grad_v[b, :, nx - 1, :, zs] = g.astype(BF16).reshape(c, yb, ZC)

    def weight_grad(b, planes_x):
        for x in planes_x:
            planes = [s_ref[b, centre(x + i)] for i in range(3)]
            right = jnp.concatenate(planes + [jnp.ones((rows, z), BF16)], axis=0)
            product = lax.dot_general(d_ref[b, pl.ds((x + 1) * 3 * rows, 3 * rows)], right, NT,
                                      preferred_element_type=F32)
            for i in range(4):
                acc_ref[i] += product[:, i * rows:(i + 1) * rows]

    def inner(b):
        for copy in load(b):
            copy.wait()
        for x in range(nx):
            fill(b, x + 1, act_v[b, :, x].reshape(rows, z))
        for x in range(1, nx - 1, 2):
            forward(b, x)
        for x in range(1, nx - 1):
            shift_delta(b, x + 1)
        weight_grad(b, range(1, nx - 1))
        begin_faces(b)

    acc_ref[...] = jnp.zeros_like(acc_ref)
    over_samples(inner)

    def outer(b):
        received_both(face, b)
        fill(b, 0, halo[0, b].reshape(rows, z))
        fill(b, nx + 1, halo[1, b].reshape(rows, z))
        end_faces(b)
        @pl.when(b < nb - 1)
        def _():
            start_both(delta(0), b)
            start_both(delta(1), b)

        shift_delta(b, 1)
        shift_delta(b, nx)
        weight_grad(b, (0, nx - 1))

    over_samples(outer)

    lane = lax.broadcasted_iota(jnp.int32, (c, rows), 1)
    row = lax.broadcasted_iota(jnp.int32, (c, rows), 0)

    def place(tap, value):
        at, col = tap // 4 * c, tap % 4 * rows
        fold_ref[at:at + c, col:col + rows] = value

    for i in range(3):
        for k in range(3):
            lines = [acc_ref[i, pl.ds(k * rows + y, c, stride=yb), :] for y in range(yb)]
            for j in range(3):
                value = jnp.zeros((c, rows), F32)
                for y in range(yb):
                    if 0 <= y + j - 1 < yb:
                        value = jnp.where(lane % yb == y + j - 1, lines[y], value)
                place((i * 3 + j) * 3 + k, value)
    total = jnp.zeros((c, rows), F32)
    for y in range(yb):
        total = total + acc_ref[3, pl.ds(rows + y, c, stride=yb), :]
    place(27, jnp.where(lane == row * yb, total, 0.0))
    r = lax.broadcasted_iota(jnp.int32, (4 * rows, 4 * c), 0)
    s = lax.broadcasted_iota(jnp.int32, (4 * rows, 4 * c), 1)
    gather = jnp.where(r // yb == s, 1.0, 0.0).astype(BF16)
    rest = fold_ref[...]
    flat = jnp.zeros((7 * c, 4 * c), F32)
    for _ in range(3):
        term = rest.astype(BF16)
        rest = rest - term.astype(F32)
        flat = flat + jnp.dot(term, gather, preferred_element_type=F32)
    size = parts.shape[2]
    for at in range(n):
        lo, hi = at * size, min((at + 1) * size, 7 * c)
        filled = max(hi - lo, 0)
        if filled:
            parts[at // chips, at % chips, 0:filled] = flat[lo:hi]
        if filled < size:
            parts[at // chips, at % chips, filled:size] = jnp.zeros((size - filled, 128), F32)
    exchange().start()

    def inner_back(b):
        for x in range(1, nx - 1, 2):
            backward(b, x)
        begin_back_faces(b)

    exchange().wait_recv()
    half[...] = parts[core] + pair[...]
    each_chip(lambda d, to, source: scatter(d, to).start())
    start_both(delta(0), nb - 1)
    over_samples(inner_back)

    def outer_back(b):
        for part in range(2):
            received_both(delta(part), b)
        shift_delta(b, 0)
        shift_delta(b, nx + 1)
        end_back_faces(b)

    each_chip(lambda d, to, source: scatter(d, to).wait_recv())
    mine[...] = ((half[chip] + jnp.sum(received[...], axis=0)) * scale).astype(BF16)
    each(lambda d, to, source: spread(d, me, to).start())
    start_both(delta(1), nb - 1)
    gathered[slot(me)] = mine[...]
    for b in range(nb):
        outer_back(b)
    each(lambda d, to, source: spread(d, source, to).wait_recv())
    sums_ref[...] = gathered[...].astype(F32)
    for b in range(nb):
        sent_both(face, b)
        for part in range(2):
            sent_both(delta(part), b)
    exchange().wait_send()
    each_chip(lambda d, to, source: scatter(d, to).wait_send())
    each(lambda d, to, source: spread(d, me, to).wait_send())


def chunk_rows(c, n):
    rows = 28 * c * c // 128
    return -(-rows // (16 * n)) * 16


def main(activations, cotangent, taps, channel_bias, n, scale):
    nb, c, nx, yb, z = activations.shape
    rows = c * yb
    size = chunk_rows(c, n)
    hbm = pl.BlockSpec(memory_space=pltpu.HBM)
    vmem = pl.BlockSpec(memory_space=pltpu.VMEM)
    dma = pltpu.SemaphoreType.DMA
    block = jax.ShapeDtypeStruct((nb, c, nx, yb, z), BF16)
    return pl.pallas_call(
        functools.partial(main_kernel, n=n, scale=scale),
        in_specs=[hbm, hbm, hbm, hbm],
        out_specs=[vmem, vmem, vmem],
        out_shape=[block, block, jax.ShapeDtypeStruct((n, size, 128), F32)],
        scratch_shapes=[
            pltpu.VMEM((nb, c, nx, yb, z), BF16),
            pltpu.VMEM((nb, c, nx, yb, z), BF16),
            pltpu.VMEM(taps.shape, BF16),
            pltpu.VMEM((1, c), F32),
            pltpu.VMEM((2, nb, c, yb, z), BF16),
            pltpu.VMEM((nb, (nx + 2) * 3 * rows, z), BF16),
            pltpu.VMEM((nb, (nx + 2) * 3 * rows, z), BF16),
            pltpu.VMEM((nb, 2, rows, z), F32),
            pltpu.VMEM((2 * rows, 12 * rows), BF16),
            pltpu.VMEM((2 * rows, 12 * rows), BF16),
            pltpu.VMEM((4, 3 * rows, rows), F32),
            pltpu.VMEM((7 * c, 4 * rows), F32),
            pltpu.VMEM((2, n // 2, size, 128), F32),
            pltpu.VMEM((n // 2, size, 128), F32),
            pltpu.VMEM((n // 2, size, 128), F32),
            pltpu.VMEM((n // 2 - 1, size, 128), F32),
            pltpu.VMEM((size, 128), BF16),
            pltpu.VMEM((n, size, 128), BF16),
            dma((2, nb)), dma((2,)), dma((2, nb)), dma((2, nb)), dma((2, nb, 2)), dma((2, nb, 2)),
            dma((2,)), dma((n // 2 - 1,)), dma((n // 2 - 1,)), dma((n - 1,)), dma((n - 1,)),
        ],
        compiler_params=pltpu.CompilerParams(
            collective_id=0, has_side_effects=True, vmem_limit_bytes=49 * 1024 * 1024),
        cost_estimate=pl.CostEstimate(flops=10 << 30, bytes_accessed=10 << 20, transcendentals=0),
        name="conv",
    )(activations, cotangent, taps, channel_bias.reshape(1, c))


def finish_kernel(activated_ref, grad_ref, sums_ref, activated_out, grad_out, kernel_out, bias_out,
                  kernel_v, bias_v, sem, small_sem):
    nb = activated_ref.shape[0]
    c = bias_v.shape[1]
    step = c // PIECES
    copies = [pltpu.make_async_copy(src.at[b, p * step:(p + 1) * step], dst.at[b, p * step:(p + 1) * step],
                                    sem.at[w, b, p])
              for b in range(nb) for p in range(PIECES)
              for w, (src, dst) in enumerate(((activated_ref, activated_out), (grad_ref, grad_out)))]
    for copy in copies:
        copy.start()
    flat = sums_ref[...].reshape(-1, 128)
    for tap in range(27):
        row, col = tap // 4 * c, tap % 4 * c
        kernel_v[tap] = flat[row:row + c, col:col + c]
    bias_v[...] = jnp.sum(flat[6 * c:7 * c, 3 * c:4 * c], axis=0, keepdims=True)
    small = (pltpu.make_async_copy(kernel_v, kernel_out, small_sem.at[0]),
             pltpu.make_async_copy(bias_v, bias_out, small_sem.at[1]))
    for copy in small:
        copy.start()
    copies.extend(small)
    for copy in copies:
        copy.wait()


def finish(activated, grad_input, sums):
    nb = activated.shape[0]
    c = activated.shape[1]
    hbm = pl.BlockSpec(memory_space=pl.ANY)
    vmem = pl.BlockSpec(memory_space=pltpu.VMEM)
    block = jax.ShapeDtypeStruct(activated.shape, BF16)
    return pl.pallas_call(
        finish_kernel,
        in_specs=[vmem, vmem, vmem],
        out_specs=[hbm, hbm, hbm, hbm],
        out_shape=[block, block, jax.ShapeDtypeStruct((27, c, c), F32), jax.ShapeDtypeStruct((1, c), F32)],
        scratch_shapes=[pltpu.VMEM((27, c, c), F32), pltpu.VMEM((1, c), F32),
                        pltpu.SemaphoreType.DMA((2, nb, PIECES)), pltpu.SemaphoreType.DMA((2,))],
        compiler_params=pltpu.CompilerParams(vmem_limit_bytes=16 * 1024 * 1024),
        cost_estimate=pl.CostEstimate(flops=1 << 20, bytes_accessed=8 << 20, transcendentals=0),
        name="finish",
    )(activated, grad_input, sums)


def per_device(activations, cotangent, kernel, channel_bias):
    nb, c, nx, yb, z = activations.shape
    n = lax.axis_size("gx")
    taps = jnp.transpose(kernel, (2, 3, 4, 0, 1)).reshape(27, c, c)
    cells = nb * nx * yb * z * n
    taps = pltpu.with_memory_space_constraint(taps, pltpu.HBM)
    channel_bias = pltpu.with_memory_space_constraint(channel_bias.reshape(1, c), pltpu.HBM)
    activated, grad_input, sums = main(activations, cotangent, taps, channel_bias, n, float(cells) ** -0.5)
    activated, grad_input, kernel_sums, bias_sums = finish(activated, grad_input, sums)
    grad_kernel = jnp.transpose(kernel_sums.reshape(3, 3, 3, c, c), (3, 4, 0, 1, 2))
    return activated, grad_input, grad_kernel, bias_sums.reshape(c)


def solution(mesh):
    placed = (P("grp", None, "gx", None, None), P("grp", None, "gx", None, None), P(), P())
    return jax.shard_map(
        per_device,
        mesh=mesh,
        in_specs=placed,
        out_specs=(
            P("grp", None, "gx", None, None),
            P("grp", None, "gx", None, None),
            P("grp", None, None, None, None),
            P("grp"),
        ),
        check_vma=False,
    )
```
